32 devices in a mesh: gx: 4 (over z), gy: 2 (over x), gz: 4 (over y, core).
Axes of the slice: x: 2, y: 2, z: 4, core: 2. Of those that a mesh axis runs over, the one named last changes fastest.
Arguments:
- loads: float32 [4, 2, 4, 1024, 128], P('gx', 'gy', 'gz'), may hold values from -12 to 12
- start: float32 [4, 2, 4, 1024, 128], P('gx', 'gy', 'gz'), may hold values from -6 to 6
- schur: float32 [4, 2, 4, 1024, 1024], P('gx', 'gy', 'gz'), may hold values from -2 to 8
- inv_local: float32 [4, 2, 4, 1024, 1024], P('gx', 'gy', 'gz'), may hold values from -1 to 3
- basis: float32 [4, 2, 4, 1024, 128], P('gx', 'gy', 'gz'), may hold values from -0.1875 to 0.1875
- coarse_inv: float32 [4096, 4096], P(('gx', 'gy')), may hold values from -0.01 to 0.07
- face_index: int32 [4, 2, 4, 6, 160], P('gx', 'gy', 'gz'), may hold values from 0 to 1023, as said below
- multiplicity: int32 [4, 2, 4, 1024], P('gx', 'gy', 'gz'), may hold values from 1 to 2, as said below
- primal_map: int32 [4, 2, 4, 128], P('gx', 'gy', 'gz'), may hold values from 0 to 4095, all different within a row
Outputs:
- solution: float32 [4, 2, 4, 1024, 128], P('gx', 'gy', 'gz')
- residual: float32 [4, 2, 4, 1024, 128], P('gx', 'gy', 'gz')
The draws below stay inside these ranges and needn't reach their ends.
Inputs may be any that keep to these rules, and one draw needn't show every extreme that they name: face_index[x, y, z, 2a + s] lists 160 distinct interface slots of subdomain (x, y, z) on its face toward the lower (s = 0) or higher (s = 1) neighbour along grid direction a; the six lists of one subdomain are disjoint. `multiplicity`: 1, plus 1 on slots listed in a face whose neighbouring subdomain lies inside the grid. `primal_map`: each subdomain lists 128 distinct primal unknowns, and every primal unknown is listed by some subdomain.
All inputs are finite; a program needn't handle non-finite values.
Results may differ from the reference program's by a relative error of at most 0.00012.
Values sent between devices are 32-bit elements; how exact they have to be, the bound alone decides.
A program may use at most 64 MiB of HBM per device.

```python
import math
import jax
import jax.numpy as jnp
from jax import lax

NI = 1024
FACE = 160
NPL = 128
NPRIM = 4096
L = 128
ITERS = 2
SX = 4
SY = 2
SZ = 4


def stiffness(key):
    return jnp.exp(jax.random.uniform(jax.random.fold_in(key, 7), (SX, SY, SZ), jnp.float32, math.log(0.5), math.log(4.0)))


def symmetric_noise(key, order, level):
    normal_draw = jax.random.normal(key, (order, order), jnp.float32)
    return (normal_draw + normal_draw.T) * (level / math.sqrt(2.0 * order))


def local_matrices(key, label, low, high, level):
    subdomains = SX * SY * SZ
    subkeys = jax.random.split(jax.random.fold_in(key, label), subdomains)

    def single(subkey):
        first_key, second_key = jax.random.split(subkey)
        diagonal = jax.random.uniform(first_key, (NI,), jnp.float32, low, high)
        return jnp.diag(diagonal) + symmetric_noise(second_key, NI, level)
    return lax.map(single, subkeys)


def draw_schur(key, part):
    matrices = local_matrices(key, 21, 0.75, 1.5, 0.3)
    scaled = matrices * stiffness(key).reshape(-1, 1, 1)
    return scaled.reshape(SX, SY, SZ, NI, NI)


def draw_inv_local(key, part):
    matrices = local_matrices(key, 22, 0.6, 1.2, 0.2)
    scaled = matrices / stiffness(key).reshape(-1, 1, 1)
    return scaled.reshape(SX, SY, SZ, NI, NI)


def draw_coarse_inv(key, part):
    first_key, second_key = jax.random.split(jax.random.fold_in(key, 23))
    diagonal = jax.random.uniform(first_key, (NPRIM,), jnp.float32, 0.03, 0.06)
    return jnp.diag(diagonal) + symmetric_noise(second_key, NPRIM, 0.01)


def face_lists(key):
    subdomains = SX * SY * SZ
    subkeys = jax.random.split(jax.random.fold_in(key, 11), subdomains)
    orders = jax.vmap(lambda subkey: jax.random.permutation(subkey, NI))(subkeys)
    return orders[:, :6 * FACE].reshape(SX, SY, SZ, 6, FACE).astype(jnp.int32)


def draw_face_index(key, part):
    return face_lists(key)


def draw_multiplicity(key, part):
    lists = face_lists(key)
    subdomains = SX * SY * SZ
    first = jnp.broadcast_to(jnp.arange(SX).reshape(SX, 1, 1), (SX, SY, SZ))
    second = jnp.broadcast_to(jnp.arange(SY).reshape(1, SY, 1), (SX, SY, SZ))
    third = jnp.broadcast_to(jnp.arange(SZ).reshape(1, 1, SZ), (SX, SY, SZ))
    exists = jnp.stack([first > 0, first < SX - 1, second > 0, second < SY - 1, third > 0, third < SZ - 1], axis=-1).astype(jnp.int32)
    flags = jnp.broadcast_to(exists[..., None], lists.shape)
    base = jnp.ones((subdomains, NI), jnp.int32)
    counted = jax.vmap(lambda rows, where, extra: rows.at[where].add(extra))(base, lists.reshape(subdomains, -1), flags.reshape(subdomains, -1))
    return counted.reshape(SX, SY, SZ, NI)


def shard_levels(key, extent, pieces, smallest, high):
    gain = 1.0
    for position, shards_of in pieces:
        draws = jax.random.uniform(jax.random.fold_in(jax.random.fold_in(key, 6), position), (shards_of,), jnp.float32, smallest / len(pieces), high / len(pieces))
        gain = gain * jnp.repeat(jnp.exp(draws), extent[position] // shards_of).reshape((-1,) + (1,) * (len(extent) - 1 - position))
    return gain


def picks_of(stream_key, rows, amount, top, lift):
    order = jax.random.permutation(jax.random.fold_in(stream_key, 1), amount)
    pull = order
    for power in range(3):
        pull = pull * pull // amount
    pull = pull * lift // amount
    tickets = jax.random.randint(jax.random.fold_in(stream_key, 2), (rows, amount), 0, 4096) + pull
    holders = jax.random.permutation(jax.random.fold_in(stream_key, 3), rows)[jnp.arange(amount) % rows]
    tickets = jnp.where(jnp.arange(rows)[:, None] == holders[None, :], 1 << 14, tickets)
    priority = tickets * amount + jnp.arange(amount)
    return lax.top_k(priority.astype(jnp.int32), top)[1].astype(jnp.int32)


def bell_draw(stream_key, shape, spread, reach, shards=(), kind=jnp.bfloat16):
    values = jax.random.normal(stream_key, shape, jnp.float32) * spread
    if len(shards) > 0:
        values = shard_levels(stream_key, shape, shards, -0.22, 0.18) * values
    return jnp.clip(values, min=-reach, max=reach).astype(kind)


def setup_inputs(seed: int = 0) -> dict:
    key_of = jax.random.split(jax.random.key(seed), 10)
    loads = bell_draw(key_of[0], (SX, SY, SZ, NI, L), 2.0, 12.0, ((0, 4), (1, 2), (2, 4)), jnp.float32)
    start = bell_draw(key_of[1], (SX, SY, SZ, NI, L), 1.0, 6.0, ((0, 4), (1, 2), (2, 4)), jnp.float32)
    schur = draw_schur(jax.random.fold_in(key_of[9], 71), 0)
    inv_local = draw_inv_local(jax.random.fold_in(key_of[9], 71), 0)
    basis = bell_draw(key_of[4], (SX, SY, SZ, NI, NPL), NI ** -0.5, 0.1875, ((0, 4), (1, 2), (2, 4)), jnp.float32)
    coarse_inv = draw_coarse_inv(jax.random.fold_in(key_of[9], 71), 0)
    face_index = draw_face_index(jax.random.fold_in(key_of[9], 71), 0)
    multiplicity = draw_multiplicity(jax.random.fold_in(key_of[9], 71), 0)
    primal_map = picks_of(key_of[8], SX * SY * SZ, NPRIM, NPL, 0).reshape((SX, SY, SZ, NPL))
    return dict(loads=loads, start=start, schur=schur, inv_local=inv_local, basis=basis, coarse_inv=coarse_inv, face_index=face_index, multiplicity=multiplicity, primal_map=primal_map)


damping = 0.6


def from_lower(array, axis):
    length = array.shape[axis]
    widths = [(0, 0)] * array.ndim
    widths[axis] = (1, 0)
    return lax.slice_in_dim(jnp.pad(array, widths), 0, length, axis=axis)


def from_upper(array, axis):
    length = array.shape[axis]
    widths = [(0, 0)] * array.ndim
    widths[axis] = (0, 1)
    return lax.slice_in_dim(jnp.pad(array, widths), 1, length + 1, axis=axis)


def interface_sum(field, face_index):
    grid = field.shape[:3]
    unknowns = field.shape[3]
    load_cases = field.shape[4]
    flat = field.reshape(-1, unknowns, load_cases)
    slots = face_index.reshape(flat.shape[0], -1)
    gathered = jax.vmap(lambda rows, where: rows[where])(flat, slots)
    face_values = gathered.reshape(grid + (6, face_index.shape[4], load_cases))
    received = []
    for axis in range(3):
        received.append(from_lower(face_values[:, :, :, 2 * axis + 1], axis))
        received.append(from_upper(face_values[:, :, :, 2 * axis], axis))
    arrived = jnp.stack(received, axis=3).reshape(flat.shape[0], -1, load_cases)
    summed = jax.vmap(lambda rows, where, extra: rows.at[where].add(extra))(flat, slots, arrived)
    return summed.reshape(field.shape)


def batched(matrices, vectors):
    return jnp.einsum('pij,pjl->pil', matrices, vectors, precision=lax.Precision.HIGHEST)


def reference(loads, start, schur, inv_local, basis, coarse_inv, face_index, multiplicity, primal_map):
    subdomains = loads.shape[0] * loads.shape[1] * loads.shape[2]
    unknowns = loads.shape[3]
    load_cases = loads.shape[4]
    flat_schur = schur.reshape(subdomains, unknowns, unknowns)
    flat_inverse = inv_local.reshape(subdomains, unknowns, unknowns)
    flat_basis = basis.reshape(subdomains, unknowns, -1)
    weight = 1.0 / multiplicity.astype(jnp.float32)[..., None]
    primal_ids = primal_map.reshape(subdomains, -1)
    solution = start
    residual = start
    for iteration in range(ITERS):
        product = batched(flat_schur, solution.reshape(subdomains, unknowns, load_cases)).reshape(loads.shape)
        residual = loads - interface_sum(product, face_index)
        weighted = (weight * residual).reshape(subdomains, unknowns, load_cases)
        local = batched(flat_inverse, weighted)
        terms = jnp.einsum('pin,pil->pnl', flat_basis, weighted, precision=lax.Precision.HIGHEST)
        coarse_load = jnp.zeros((coarse_inv.shape[0], load_cases), jnp.float32).at[primal_ids.reshape(-1)].add(terms.reshape(-1, load_cases))
        coarse_sol = jnp.dot(coarse_inv, coarse_load, precision=lax.Precision.HIGHEST, preferred_element_type=jnp.float32)
        correction = batched(flat_basis, coarse_sol[primal_ids])
        update = interface_sum(weight * (local + correction).reshape(loads.shape), face_index)
        solution = solution + damping * update
    return solution, residual
```

```python
import functools
import itertools

import jax
import jax.numpy as jnp
from jax import lax
from jax.experimental import pallas as pl
from jax.experimental.pallas import tpu as pltpu
from jax.sharding import PartitionSpec as P

ITERS = 2
damping = 0.6
MESH = pl.DeviceIdType.MESH
AXES = ("gx", "gy", "gz")


class Grid:
    def __init__(self, sizes):
        self.sizes = sizes
        gx, gy, gz = sizes
        self.lo = 2 if gz % 2 == 0 else 1
        self.hi = gz // self.lo
        self.stages = (gx, gy, self.hi, self.lo)
        self.count = gx * gy * gz
        self.c = tuple(lax.axis_index(a) for a in AXES)
        self.place = (self.c[0], self.c[1], self.c[2] // self.lo, self.c[2] % self.lo)

    def linear(self, place):
        x, y, h, l = place
        return (x * self.sizes[1] + y) * self.sizes[2] + h * self.lo + l

    def device(self, place):
        x, y, h, l = place
        return (x, y, h * self.lo + l)

    def others(self, function):
        gx, gy, gz = self.sizes
        me = self.linear(self.place)

        def step(delta, carry):
            t = (me + delta) % self.count
            function((t // (gy * gz), (t // gz) % gy, t % gz))
            return carry

        lax.fori_loop(1, self.count, step, 0)

    def announce(self):
        semaphore = pltpu.get_barrier_semaphore()
        self.others(
            lambda target: pl.semaphore_signal(
                semaphore, inc=1, device_id=target, device_id_type=MESH
            )
        )

    def meet(self):
        if self.count > 1:
            pl.semaphore_wait(pltpu.get_barrier_semaphore(), self.count - 1)


class Gather:
    def __init__(self, grid, buffer, whole, band, order, send, recv):
        self.grid, self.buffer, self.whole, self.band = grid, buffer, whole, band
        self.order, self.send, self.recv = order, send, recv
        self.lengths = tuple(grid.stages[o] for o in order)

    def place(self, offset):
        g = self.grid
        place = list(g.place)
        for o, d in zip(self.order, offset):
            if d:
                place[o] = (g.place[o] + g.stages[o] - d) % g.stages[o]
        return place

    def block(self, offset):
        first = self.grid.linear(self.place(offset)) * self.whole + self.band[0]
        return self.buffer.at[pl.ds(pl.multiple_of(first, 8), self.band[1])]

    def number(self, offset):
        value = 0
        for d, n in zip(offset, self.lengths):
            value = value * n + d
        return value

    def forward(self, offset, first):
        for stage in range(first, 4):
            for delta in range(1, self.lengths[stage]):
                back = [0, 0, 0, 0]
                back[stage] = self.lengths[stage] - delta
                arrived = list(offset)
                arrived[stage] = delta
                k = self.number(arrived)
                block = self.block(offset)
                c = pltpu.make_async_remote_copy(
                    src_ref=block, dst_ref=block, send_sem=self.send,
                    recv_sem=self.recv.at[k], device_id=self.grid.device(self.place(back)),
                    device_id_type=MESH,
                )
                c.start()

    def start(self):
        self.forward((0, 0, 0, 0), 0)

    def finish(self, stage):
        for head in itertools.product(*[range(n) for n in self.lengths[:stage]]):
            for delta in range(1, self.lengths[stage]):
                arrived = tuple(head) + (delta,) + (0,) * (3 - stage)
                block = self.block(arrived)
                k = self.number(arrived)
                pltpu.make_async_remote_copy(
                    src_ref=block, dst_ref=block, send_sem=self.send,
                    recv_sem=self.recv.at[k], device_id=self.grid.c, device_id_type=MESH,
                ).wait_recv()
                self.forward(arrived, stage + 1)

    def drain(self):
        if self.grid.count > 1:
            block = self.buffer.at[pl.ds(0, (self.grid.count - 1) * self.band[1])]
            pltpu.make_async_remote_copy(
                src_ref=block, dst_ref=block, send_sem=self.send, recv_sem=self.recv.at[0],
                device_id=self.grid.c, device_id_type=MESH,
            ).wait_send()


class Halves:
    def __init__(self, grid, buffer, rows, send, recv):
        half = rows // 2
        self.parts = [
            Gather(grid, buffer, rows, (i * half, half), order, send.at[i], recv.at[i])
            for i, order in enumerate(((0, 1, 2, 3), (0, 2, 1, 3)))
        ]

    def start(self):
        for part in self.parts:
            part.start()

    def finish(self, work=()):
        work = list(work)
        for stage in range(4):
            for part in self.parts:
                part.finish(stage)
                if work:
                    work.pop(0)()
        for rest in work:
            rest()

    def drain(self):
        for part in self.parts:
            part.drain()


def split(value):
    high = value.astype(jnp.bfloat16)
    low = (value - high.astype(jnp.float32)).astype(jnp.bfloat16)
    return high, low


def tile_of(total, want):
    while total % want:
        want //= 2
    return want


def split_rows(source, high, low):
    rows = source.shape[0]
    tile = tile_of(rows, 64)

    def step(i, carry):
        r = pl.ds(pl.multiple_of(i * tile, tile), tile)
        h, l = split(source[r, :])
        high[r, :] = h
        low[r, :] = l
        return carry

    lax.fori_loop(0, rows // tile, step, 0)


def split_beside(source, both):
    rows, width = source.shape
    tile = tile_of(rows, 128)

    def step(i, carry):
        r = pl.ds(pl.multiple_of(i * tile, tile), tile)
        h, l = split(source[r, :])
        both[r, 0:width] = h
        both[r, width : 2 * width] = l
        return carry

    lax.fori_loop(0, rows // tile, step, 0)


def product(high, low, both):
    width = both.shape[1] // 2
    wide = jnp.dot(high, both[...], preferred_element_type=jnp.float32)
    thin = jnp.dot(low, both[:, 0:width], preferred_element_type=jnp.float32)
    return wide[:, 0:width] + wide[:, width:] + thin


def by_rows(rows, want, function):
    tile = tile_of(rows, want)

    def step(i, carry):
        function(pl.ds(pl.multiple_of(i * tile, tile), tile))
        return carry

    lax.fori_loop(0, rows // tile, step, 0)


def take_rows(target, source, index, count):
    unroll = tile_of(count, 32)

    def step(i, carry):
        first = pl.multiple_of(i * unroll, unroll)
        for j in range(unroll):
            target[pl.ds(first + j, 1), :] = source[pl.ds(index(first + j), 1), :]
        return carry

    lax.fori_loop(0, count // unroll, step, 0)


def main_kernel(
    sizes, face,
    slots, slot_rows, multiplicity, own_map,
    loads_in, start_in, basis_in, schur, inverse, coarse_inv,
    solution_out, residual_out,
    full, s_high, s_low, b_high, b_low, m_high, m_low, t_high, t_low, p_high, p_low, n_high, n_low,
    c_high, c_low, coarse_own, coarse_t, map_all, all_map, picked, spread,
    loads, solution, basis, weight, residual, field, local, early, both, edge_both, term_both, sol_both, coarse_rows, corrected,
    faces, arrived, term_all, sol_all,
    load_sem, out_sem, map_send, map_recv, face_send, face_recv, term_send, term_recv, sol_send, sol_recv,
):
    grid = Grid(sizes)
    unknowns, cases = solution.shape
    primal = basis.shape[1]
    own = coarse_t.shape[1]
    edge = corrected.shape[0]
    shape_turn = 2 * ITERS
    first_own = pl.multiple_of(grid.c[2] * own, own)

    def load(k, source, target):
        return pltpu.make_async_copy(source, target, load_sem.at[k])

    load_x = load(0, start_in, solution)
    load_s = load(1, schur, full)
    load_m = load(2, basis_in, basis)
    load_l = load(3, loads_in, loads)
    load_c = load(4, coarse_inv.at[pl.ds(first_own, own)], coarse_own)
    load_b = load(5, inverse, full)
    for each in (load_x, load_s, load_m, load_l, load_c):
        each.start()
    for landing in arrived:
        landing[...] = jnp.zeros_like(landing)
    with jax.named_scope("announce"):
        grid.announce()

    me = grid.linear(grid.place)
    map_all[me] = own_map[...]

    with jax.named_scope("splitx"):
        load_x.wait()
        split_beside(solution, both)
    with jax.named_scope("waits"):
        load_s.wait()
    with jax.named_scope("splits"):
        split_rows(full, s_high, s_low)
    load_b.start()

    def stiff(r):
        field[r, :] = product(s_high[r, :], s_low[r, :], both)

    with jax.named_scope("stiff"):
        by_rows(unknowns, 256, stiff)

    def face_copy(turn, d):
        axis, side = d // 2, d % 2
        target = list(grid.c)
        target[axis] = grid.c[axis] + (1 if side else -1)
        return pltpu.make_async_remote_copy(
            src_ref=faces.at[turn, pl.ds(d * face, face)],
            dst_ref=arrived[turn].at[pl.ds((d ^ 1) * face, face)],
            send_sem=face_send.at[turn, d],
            recv_sem=face_recv.at[turn, d ^ 1],
            device_id=tuple(target), device_id_type=MESH,
        )

    def exists(d):
        axis, side = d // 2, d % 2
        return grid.c[axis] < sizes[axis] - 1 if side else grid.c[axis] > 0

    def collect(turn, source, d):
        take_rows(faces.at[turn, pl.ds(d * face, face)], source, lambda k: slots[d, k], face)

    def dispatch(turn, d):
        @pl.when(exists(d))
        def _():
            face_copy(turn, d).start()

    def exchange_start(turn, source):
        for d in range(6):
            collect(turn, source, d)
            dispatch(turn, d)

    def exchange_wait(turn):
        for d in range(6):

            @pl.when(exists(d))
            def _():
                block = arrived[turn].at[pl.ds(d * face, face)]
                pltpu.make_async_remote_copy(
                    src_ref=block, dst_ref=block, send_sem=face_send.at[turn, d],
                    recv_sem=face_recv.at[turn, d], device_id=grid.c, device_id_type=MESH,
                ).wait_recv()

    def exchange_drain(turn):
        for d in range(6):

            @pl.when(exists(d))
            def _():
                face_copy(turn, d).wait_send()

    with jax.named_scope("basis"):
        load_m.wait()
        for k in range(0, unknowns, 128):
            r = slice(k, k + 128)
            inverse_count = 1.0 / multiplicity[:, r].astype(jnp.float32)
            weight[r, :] = jnp.broadcast_to(inverse_count, (cases, 128)).T
            scaled = weight[r, 0:1] * basis[r, :]
            basis[r, :] = scaled
            h, l = split(scaled)
            m_high[r, :] = h
            m_low[r, :] = l
            h, l = split(scaled.T)
            t_high[:, r] = h
            t_low[:, r] = l
    with jax.named_scope("collect0"):
        for d in range(6):
            collect(0, field, d)
    with jax.named_scope("psi"):
        shape_edges = faces.at[shape_turn]
        for d in range(6):
            collect(shape_turn, basis, d)
        if edge > 6 * face:
            shape_edges[6 * face : edge, :] = jnp.zeros((edge - 6 * face, cases), jnp.float32)
        for k in range(0, edge, 128):
            h, l = split(shape_edges[k : k + 128, :].T)
            p_high[:, k : k + 128] = h
            p_low[:, k : k + 128] = l
    with jax.named_scope("meet"):
        grid.meet()
    with jax.named_scope("dispatch"):
        for d in range(6):
            dispatch(0, d)
        for d in range(6):
            dispatch(shape_turn, d)

        def map_copy(target):
            return pltpu.make_async_remote_copy(
                src_ref=map_all.at[me], dst_ref=map_all.at[me], send_sem=map_send, recv_sem=map_recv,
                device_id=target, device_id_type=MESH,
            )

        grid.others(lambda target: map_copy(target).start())
    with jax.named_scope("spread"):
        hits = slot_rows[...]
        tile = tile_of(unknowns, 64)

        def mark(i, carry):
            r = pl.ds(pl.multiple_of(i * tile, tile), tile)
            row = lax.broadcasted_iota(jnp.int32, (tile, edge), 0) + i * tile
            spread[r, :] = jnp.where(row == hits, 1.0, 0.0).astype(jnp.bfloat16)
            return carry

        lax.fori_loop(0, unknowns // tile, mark, 0)
        corrected[...] = jnp.zeros_like(corrected)

    def moved(r):
        wide = jnp.dot(spread[r, :], edge_both[...], preferred_element_type=jnp.float32)
        return wide[:, 0:cases] + wide[:, cases : 2 * cases]

    def neighbour(d):
        axis, side = d // 2, d % 2
        stride = (sizes[1] * sizes[2], sizes[2], 1)[axis]
        step = (grid.c[axis] + (1 if side else -1) + sizes[axis]) % sizes[axis] - grid.c[axis]
        return me + step * stride

    gathers = []
    for iteration in range(ITERS):
        turn = 2 * iteration
        slot = iteration % term_all.shape[0]
        if slot < iteration:
            gathers.pop(0).drain()
        if iteration:
            with jax.named_scope("splitx"):
                split_beside(solution, both)
            with jax.named_scope("stiff"):
                by_rows(unknowns, 256, stiff)
            with jax.named_scope("xstart"):
                exchange_start(turn, field)
        else:
            load_l.wait()

        def before(r):
            value = loads[r, :] - field[r, :]
            field[r, :] = value
            h, l = split(value)
            both[r, 0:cases] = h
            both[r, cases : 2 * cases] = l

        with jax.named_scope("before"):
            by_rows(unknowns, 128, before)
            early[...] = product(t_high[...], t_low[...], both)
        if iteration == 0:
            with jax.named_scope("splitb"):
                load_b.wait()
                split_rows(full, b_high, b_low)
            with jax.named_scope("transc"):
                load_c.wait()
                for k in range(0, coarse_own.shape[1], 128):
                    coarse_t[k : k + 128, :] = coarse_own[:, k : k + 128].T
        with jax.named_scope("xwait"):
            exchange_wait(turn)
        with jax.named_scope("term"):
            split_beside(arrived[turn], edge_both)
            mine = pl.multiple_of(me * primal, primal)
            term_all[slot, pl.ds(mine, primal), :] = early[...] - product(p_high[...], p_low[...], edge_both)
        terms = Halves(grid, term_all.at[slot], primal, term_send.at[iteration], term_recv.at[iteration])
        with jax.named_scope("termstart"):
            terms.start()
        gathers.append(terms)

        def settle(r):
            value = field[r, :] - moved(r)
            residual[r, :] = value
            h, l = split(weight[r, :] * value)
            both[r, 0:cases] = h
            both[r, cases : 2 * cases] = l

        with jax.named_scope("settle"):
            by_rows(unknowns, 256, settle)
        if iteration == ITERS - 1:
            out_residual = pltpu.make_async_copy(residual, residual_out, out_sem.at[0])
            out_residual.start()

        def invert(r):
            local[r, :] = weight[r, :] * product(b_high[r, :], b_low[r, :], both)

        with jax.named_scope("invert"):
            by_rows(unknowns, 256, invert)
        with jax.named_scope("xlocal"):
            exchange_start(turn + 1, local)

        def read_maps():
            with jax.named_scope("maps"):
                if grid.count > 1:
                    block = map_all.at[pl.ds(0, grid.count - 1)]
                    pltpu.make_async_remote_copy(
                        src_ref=block, dst_ref=block, send_sem=map_send, recv_sem=map_recv,
                        device_id=grid.c, device_id_type=MESH,
                    ).wait()
                to_scalars = pltpu.make_async_copy(map_all, all_map, load_sem.at[6])
                to_scalars.start()
                to_scalars.wait()

        def pick(p, carry):
            take_rows(picked, coarse_t, lambda k: all_map[p, 0, k], primal)
            h, l = split(picked[...].T)
            k = pl.ds(pl.multiple_of(p * primal, primal), primal)
            c_high[:, k] = h
            c_low[:, k] = l
            return carry

        def picks(lower, upper):
            def run():
                with jax.named_scope("pick"):
                    lax.fori_loop(lower, upper, pick, 0)

            return run

        def shapes():
            with jax.named_scope("shapes"):
                exchange_wait(shape_turn)
                split_rows(arrived[shape_turn], n_high, n_low)

        work = []
        if iteration == 0:
            parts = 4
            bounds = [grid.count * k // parts for k in range(parts + 1)]
            work = [read_maps] + [picks(bounds[k], bounds[k + 1]) for k in range(parts)] + [shapes]
        with jax.named_scope("termfin"):
            terms.finish(work)
        mine = pl.multiple_of(me * own, own)
        coarse_tile = term_both.shape[0]
        sol_all[iteration][pl.ds(mine, own), :] = jnp.zeros((own, cases), jnp.float32)

        def coarse(i, carry):
            k = pl.ds(pl.multiple_of(i * coarse_tile, coarse_tile), coarse_tile)
            split_beside(term_all.at[slot, k], term_both)
            sol_all[iteration][pl.ds(mine, own), :] += product(c_high[:, k], c_low[:, k], term_both)
            return carry

        with jax.named_scope("coarse"):
            lax.fori_loop(0, grid.count * primal // coarse_tile, coarse, 0)
        sols = Halves(grid, sol_all[iteration], own, sol_send.at[iteration], sol_recv.at[iteration])
        with jax.named_scope("solstart"):
            sols.start()
        gathers.append(sols)

        with jax.named_scope("xlwait"):
            exchange_wait(turn + 1)

        def approach(r):
            solution[r, :] = solution[r, :] + damping * (local[r, :] + moved(r))

        with jax.named_scope("approach"):
            split_beside(arrived[turn + 1], edge_both)
            by_rows(unknowns, 256, approach)
        with jax.named_scope("solfin"):
            sols.finish()
        with jax.named_scope("take"):
            take_rows(coarse_rows, sol_all[iteration], lambda k: all_map[me, 0, k], primal)
            split_beside(coarse_rows, sol_both)
            for d in range(6):
                q = neighbour(d)
                r = slice(d * face, (d + 1) * face)
                take_rows(coarse_rows, sol_all[iteration], lambda k: all_map[q, 0, k], primal)
                split_beside(coarse_rows, term_both.at[0:primal])
                corrected[r, :] = product(n_high[r, :], n_low[r, :], term_both.at[0:primal])
            split_beside(corrected, edge_both)

        def advance(r):
            change = product(m_high[r, :], m_low[r, :], sol_both) + moved(r)
            solution[r, :] = solution[r, :] + damping * change

        with jax.named_scope("advance"):
            by_rows(unknowns, 256, advance)
    with jax.named_scope("out"):
        out_solution = pltpu.make_async_copy(solution, solution_out, out_sem.at[1])
        out_solution.start()
        for turn in range(2 * ITERS + 1):
            exchange_drain(turn)
        for gather in gathers:
            gather.drain()
        out_residual.wait()
        out_solution.wait()


def body(sizes, loads, start, schur, inv_local, basis, coarse_inv, face_index, multiplicity, primal_map):
    unknowns, cases = loads.shape[3:]
    face = face_index.shape[4]
    primal = basis.shape[4]
    count = sizes[0] * sizes[1] * sizes[2]
    total = coarse_inv.shape[1]
    own = coarse_inv.shape[0] // sizes[2]
    edge = -(-6 * face // 128) * 128
    vmem = pl.BlockSpec(memory_space=pltpu.VMEM)
    smem = pl.BlockSpec(memory_space=pltpu.SMEM)
    anywhere = pl.BlockSpec(memory_space=pl.ANY)
    dma = pltpu.SemaphoreType.DMA
    f32, bf16 = jnp.float32, jnp.bfloat16
    turns = 2 * ITERS + 1
    coarse_tile = tile_of(count * primal, 1024)
    term_slots = ITERS if ITERS * count * primal <= 8 * unknowns else 1
    vec = pltpu.VMEM((unknowns, cases), f32)
    out = jax.ShapeDtypeStruct((unknowns, cases), f32)
    lists = face_index.reshape(6, face)
    row = jnp.pad(lists.reshape(1, 6 * face), ((0, 0), (0, edge - 6 * face)), constant_values=-1)
    solution, residual = pl.pallas_call(
        functools.partial(main_kernel, sizes, face),
        out_shape=(out, out),
        in_specs=[smem] + [vmem] * 3 + [anywhere] * 6,
        out_specs=(anywhere, anywhere),
        scratch_shapes=[
            pltpu.VMEM((unknowns, unknowns), f32),
            pltpu.VMEM((unknowns, unknowns), bf16),
            pltpu.VMEM((unknowns, unknowns), bf16),
            pltpu.VMEM((unknowns, unknowns), bf16),
            pltpu.VMEM((unknowns, unknowns), bf16),
            pltpu.VMEM((unknowns, primal), bf16),
            pltpu.VMEM((unknowns, primal), bf16),
            pltpu.VMEM((primal, unknowns), bf16),
            pltpu.VMEM((primal, unknowns), bf16),
            pltpu.VMEM((primal, edge), bf16),
            pltpu.VMEM((primal, edge), bf16),
            pltpu.VMEM((edge, primal), bf16),
            pltpu.VMEM((edge, primal), bf16),
            pltpu.VMEM((own, count * primal), bf16),
            pltpu.VMEM((own, count * primal), bf16),
            pltpu.VMEM((own, total), f32),
            pltpu.VMEM((total, own), f32),
            pltpu.VMEM((count, 1, primal), jnp.int32),
            pltpu.SMEM((count, 1, primal), jnp.int32),
            pltpu.VMEM((primal, own), f32),
            pltpu.VMEM((unknowns, edge), bf16),
            vec, vec, pltpu.VMEM((unknowns, primal), f32), vec, vec, vec, vec,
            pltpu.VMEM((primal, cases), f32),
            pltpu.VMEM((unknowns, 2 * cases), bf16),
            pltpu.VMEM((edge, 2 * cases), bf16),
            pltpu.VMEM((coarse_tile, 2 * cases), bf16),
            pltpu.VMEM((primal, 2 * cases), bf16),
            pltpu.VMEM((primal, cases), f32),
            pltpu.VMEM((edge, cases), f32),
            pltpu.VMEM((turns, edge, cases), f32),
            [pltpu.VMEM((edge, cases), f32) for _ in range(turns)],
            pltpu.VMEM((term_slots, count * primal, cases), f32),
            [pltpu.VMEM((total, cases), f32) for _ in range(ITERS)],
            dma((7,)), dma((2,)),
            dma(()), dma(()),
            dma((turns, 6)), dma((turns, 6)),
            dma((ITERS, 2)), dma((ITERS, 2, count)),
            dma((ITERS, 2)), dma((ITERS, 2, count)),
        ],
        compiler_params=pltpu.CompilerParams(
            collective_id=1, has_side_effects=True, vmem_limit_bytes=67043328
        ),
    )(
        lists, row, multiplicity.reshape(1, unknowns), primal_map.reshape(1, primal),
        loads.reshape(unknowns, cases), start.reshape(unknowns, cases), basis.reshape(unknowns, primal),
        schur.reshape(unknowns, unknowns), inv_local.reshape(unknowns, unknowns), coarse_inv,
    )
    return (solution.reshape(loads.shape), residual.reshape(loads.shape))


def solution(mesh):
    sizes = tuple(mesh.shape[a] for a in AXES)
    field = P("gx", "gy", "gz", None, None)
    placed = (field,) * 5 + (P(("gx", "gy"), None), field, P("gx", "gy", "gz", None), P("gx", "gy", "gz", None))
    return jax.shard_map(
        functools.partial(body, sizes),
        mesh=mesh,
        in_specs=placed,
        out_specs=(field, field),
        check_vma=False,
    )
```

```python
import functools
import itertools

import jax
import jax.numpy as jnp
from jax import lax
from jax.experimental import pallas as pl
from jax.experimental.pallas import tpu as pltpu
from jax.sharding import PartitionSpec as P

ITERS = 2
damping = 0.6
MESH = pl.DeviceIdType.MESH
AXES = ("gx", "gy", "gz")


def stages_of(sizes):
    gx, gy, gz = sizes
    lo = 2 if gz % 2 == 0 else 1
    return (gx, gy, gz // lo, lo)


class Grid:
    def __init__(self, sizes):
        self.sizes = sizes
        gx, gy, gz = sizes
        self.stages = stages_of(sizes)
        self.hi, self.lo = self.stages[2:]
        self.count = gx * gy * gz
        self.c = tuple(lax.axis_index(a) for a in AXES)
        self.place = (self.c[0], self.c[1], self.c[2] // self.lo, self.c[2] % self.lo)

    def linear(self, place):
        x, y, h, l = place
        return (x * self.sizes[1] + y) * self.sizes[2] + h * self.lo + l

    def device(self, place):
        x, y, h, l = place
        return (x, y, h * self.lo + l)

    def others(self, function):
        along = [[(c + d) % n for d in range(n)] for c, n in zip(self.c, self.sizes)]
        for target in list(itertools.product(*along))[1:]:
            function(target)

    def announce(self):
        semaphore = pltpu.get_barrier_semaphore()
        self.others(
            lambda target: pl.semaphore_signal(
                semaphore, inc=1, device_id=target, device_id_type=MESH
            )
        )

    def meet(self):
        if self.count > 1:
            pl.semaphore_wait(pltpu.get_barrier_semaphore(), self.count - 1)


class Gather:
    def __init__(self, grid, buffer, whole, band, order, send, recv):
        self.grid, self.buffer, self.whole, self.band = grid, buffer, whole, band
        self.order, self.send, self.recv = order, send, recv
        self.lengths = tuple(grid.stages[o] for o in order)

    def place(self, offset):
        g = self.grid
        place = list(g.place)
        for o, d in zip(self.order, offset):
            if d:
                place[o] = (g.place[o] + g.stages[o] - d) % g.stages[o]
        return place

    def block(self, offset):
        first = self.grid.linear(self.place(offset)) * self.whole + self.band[0]
        return self.buffer.at[pl.ds(pl.multiple_of(first, 8), self.band[1])]

    def number(self, offset):
        if offset[3]:
            return arrivals(self.lengths) - self.lengths[0] + offset[0]
        value = 0
        for d, n in zip(offset[:3], self.lengths[:3]):
            value = value * n + d
        return value - 1

    def copy(self, block, k, target):
        return pltpu.make_async_remote_copy(
            src_ref=block, dst_ref=block, send_sem=self.send, recv_sem=self.recv.at[k],
            device_id=target, device_id_type=MESH,
        )

    def forward(self, offset, first):
        for stage in range(first, 4):
            for delta in range(1, self.lengths[stage]):
                back = [0, 0, 0, 0]
                back[stage] = self.lengths[stage] - delta
                arrived = list(offset)
                arrived[stage] = delta
                self.copy(
                    self.block(offset), self.number(arrived), self.grid.device(self.place(back))
                ).start()

    def start(self):
        self.forward((0, 0, 0, 0), 0)

    def finish(self, stage, heads=None, idle=None):
        for head in itertools.product(*[range(n) for n in self.lengths[:stage]]):
            if heads is not None and head[0] != heads:
                continue
            for delta in range(1, self.lengths[stage]):
                arrived = tuple(head) + (delta,) + (0,) * (3 - stage)
                self.copy(self.block(arrived), self.number(arrived), self.grid.c).wait_recv()
                self.forward(arrived, stage + 1)
                if idle:
                    idle()

    def close(self, head):
        n = self.lengths
        rows = n[1] * n[2] * (n[3] - 1) * self.band[1]
        if rows:
            block = self.buffer.at[pl.ds(0, rows)]
            self.copy(block, self.number((head, 0, 0, 1)), self.grid.c).wait_recv()

    def drain(self):
        if self.grid.count > 1:
            block = self.buffer.at[pl.ds(0, (self.grid.count - 1) * self.band[1])]
            self.copy(block, 0, self.grid.c).wait_send()


def arrivals(lengths):
    return lengths[0] * lengths[1] * lengths[2] - 1 + lengths[0]


class Halves:
    def __init__(self, grid, buffer, rows, send, recv):
        half = rows // 2
        self.heads = grid.stages[0]
        self.parts = [
            Gather(grid, buffer, rows, (i * half, half), order, send.at[i], recv.at[i])
            for i, order in enumerate(((0, 1, 2, 3), (0, 2, 1, 3)))
        ]

    def start(self):
        for part in self.parts:
            part.start()

    def finish(self, first=(), work=(), after=None):
        first, work = list(first), list(work)

        def idle():
            if first or work:
                (first or work).pop(0)()

        for stage in range(2):
            for part in self.parts:
                part.finish(stage, None, idle)

        def close(head):
            for part in self.parts:
                part.close(head)
            while first:
                idle()
            if after:
                after(head)

        for head in range(self.heads):
            for part in self.parts:
                part.finish(2, head, idle)
            if head:
                close(head - 1)
        while first or work:
            idle()
        close(self.heads - 1)

    def drain(self):
        for part in self.parts:
            part.drain()


def split(value):
    high = value.astype(jnp.bfloat16)
    low = (value - high.astype(jnp.float32)).astype(jnp.bfloat16)
    return high, low


def tile_of(total, want):
    while total % want:
        want //= 2
    return want


def split_rows(source, high, low):
    rows = source.shape[0]
    tile = tile_of(rows, 64)

    def step(i, carry):
        r = pl.ds(pl.multiple_of(i * tile, tile), tile)
        h, l = split(source[r, :])
        high[r, :] = h
        low[r, :] = l
        return carry

    lax.fori_loop(0, rows // tile, step, 0)


def split_beside(source, both):
    rows, width = source.shape
    tile = tile_of(rows, 128)

    def step(i, carry):
        r = pl.ds(pl.multiple_of(i * tile, tile), tile)
        h, l = split(source[r, :])
        both[r, 0:width] = h
        both[r, width : 2 * width] = l
        return carry

    lax.fori_loop(0, rows // tile, step, 0)


def product(high, low, both):
    width = both.shape[1] // 2
    wide = jnp.dot(high, both[...], preferred_element_type=jnp.float32)
    thin = jnp.dot(low, both[:, 0:width], preferred_element_type=jnp.float32)
    return wide[:, 0:width] + wide[:, width:] + thin


def by_rows(rows, want, function):
    tile = tile_of(rows, want)

    def step(i, carry):
        function(pl.ds(pl.multiple_of(i * tile, tile), tile))
        return carry

    lax.fori_loop(0, rows // tile, step, 0)


def take_rows(target, source, index, count):
    unroll = tile_of(count, 32)

    def step(i, carry):
        first = pl.multiple_of(i * unroll, unroll)
        for j in range(unroll):
            target[pl.ds(first + j, 1), :] = source[pl.ds(index[first + j], 1), :]
        return carry

    lax.fori_loop(0, count // unroll, step, 0)


def main_kernel(
    sizes, face,
    lists_in, multiplicity_in, own_map_in,
    loads_in, start_in, basis_in, schur, inverse, coarse_inv,
    solution_out, residual_out,
    slots, slot_lists, multiplicity, full, s_high, s_low, b_high, b_low, m_high, m_low, t_high, t_low, p_high, p_low, n_high, n_low,
    c_high, c_low, coarse_own, coarse_t, map_all, all_map, picked, slot_rows, spread,
    loads, solution, basis, weight, residual, field, local, early, both, edge_both, term_both, sol_both, coarse_rows, corrected,
    faces, arrived, term_all, sol_all,
    load_sem, out_sem, map_send, map_recv, face_send, face_recv, term_send, term_recv, sol_send, sol_recv,
):
    grid = Grid(sizes)
    unknowns, cases = solution.shape
    primal = basis.shape[1]
    own = coarse_t.shape[1]
    edge = corrected.shape[0]
    shape_turn = 2
    first_own = pl.multiple_of(grid.c[2] * own, own)

    def load(k, source, target):
        return pltpu.make_async_copy(source, target, load_sem.at[k])

    load_x = load(0, start_in, solution)
    chunk = tile_of(unknowns, 256)
    chunks = unknowns // chunk
    load_s = [
        load(7 + i, schur.at[pl.ds(i * chunk, chunk)], full.at[pl.ds(i * chunk, chunk)]) for i in range(chunks)
    ]
    load_m = load(2, basis_in, basis)
    load_l = load(3, loads_in, loads)
    load_c = load(4, coarse_inv.at[pl.ds(first_own, own)], coarse_own)
    load_b = load(5, inverse, full)
    load_i = [
        load(7 + chunks, lists_in, slots), load(8 + chunks, lists_in, slot_lists),
        load(9 + chunks, multiplicity_in, multiplicity),
    ]
    me = grid.linear(grid.place)
    load_o = load(10 + chunks, own_map_in, map_all.at[me])
    for each in (load_x, *load_s, *load_i, load_o, load_m, load_l, load_c):
        each.start()
    for landing in arrived:
        landing[...] = jnp.zeros_like(landing)
    with jax.named_scope("announce"):
        grid.announce()

    with jax.named_scope("splitx"):
        load_x.wait()
        split_beside(solution, both)

    def stiff(r):
        field[r, :] = product(s_high[r, :], s_low[r, :], both)

    with jax.named_scope("stiff0"):
        for i in range(chunks):
            r = pl.ds(i * chunk, chunk)
            load_s[i].wait()
            split_rows(full.at[r], s_high.at[r], s_low.at[r])
            stiff(r)
    load_b.start()

    def face_copy(turn, d):
        axis, side = d // 2, d % 2
        target = list(grid.c)
        target[axis] = grid.c[axis] + (1 if side else -1)
        return pltpu.make_async_remote_copy(
            src_ref=faces.at[turn, pl.ds(d * face, face)],
            dst_ref=arrived[turn].at[pl.ds((d ^ 1) * face, face)],
            send_sem=face_send.at[turn, d],
            recv_sem=face_recv.at[turn, d ^ 1],
            device_id=tuple(target), device_id_type=MESH,
        )

    def exists(d):
        axis, side = d // 2, d % 2
        return grid.c[axis] < sizes[axis] - 1 if side else grid.c[axis] > 0

    def collect(turn, source, d):
        take_rows(faces.at[turn, pl.ds(d * face, face)], source, slots.at[d, 0], face)

    def dispatch(turn, d):
        @pl.when(exists(d))
        def _():
            face_copy(turn, d).start()

    def exchange_start(turn, source):
        for d in range(6):
            collect(turn, source, d)
            dispatch(turn, d)

    def exchange_wait(turn):
        for d in range(6):

            @pl.when(exists(d))
            def _():
                block = arrived[turn].at[pl.ds(d * face, face)]
                pltpu.make_async_remote_copy(
                    src_ref=block, dst_ref=block, send_sem=face_send.at[turn, d],
                    recv_sem=face_recv.at[turn, d], device_id=grid.c, device_id_type=MESH,
                ).wait_recv()

    def exchange_drain(turn):
        for d in range(6):

            @pl.when(exists(d))
            def _():
                face_copy(turn, d).wait_send()

    with jax.named_scope("collect"):
        for each in (*load_i, load_o):
            each.wait()
        collect(0, field, 0)
    with jax.named_scope("meet"):
        grid.meet()
    with jax.named_scope("xstart"):
        dispatch(0, 0)
        for d in range(1, 6):
            collect(0, field, d)
            dispatch(0, d)
    with jax.named_scope("mapsend"):

        def map_copy(target):
            return pltpu.make_async_remote_copy(
                src_ref=map_all.at[me], dst_ref=map_all.at[me], send_sem=map_send, recv_sem=map_recv,
                device_id=target, device_id_type=MESH,
            )

        grid.others(lambda target: map_copy(target).start())
    with jax.named_scope("basis"):
        load_m.wait()
        for k in range(0, unknowns, 128):
            r = slice(k, k + 128)
            inverse_count = 1.0 / multiplicity[:, r].astype(jnp.float32)
            weight[r, :] = jnp.broadcast_to(inverse_count, (cases, 128)).T
            scaled = weight[r, 0:1] * basis[r, :]
            basis[r, :] = scaled
            h, l = split(scaled)
            m_high[r, :] = h
            m_low[r, :] = l
            h, l = split(scaled.T)
            t_high[:, r] = h
            t_low[:, r] = l
    with jax.named_scope("psi"):
        for d in range(6):
            collect(shape_turn, basis, d)
        shape_edges = faces.at[shape_turn]
        if edge > 6 * face:
            shape_edges[6 * face : edge, :] = jnp.zeros((edge - 6 * face, cases), jnp.float32)
        for k in range(0, edge, 128):
            h, l = split(shape_edges[k : k + 128, :].T)
            p_high[:, k : k + 128] = h
            p_low[:, k : k + 128] = l
    for d in range(6):
        dispatch(shape_turn, d)

    def moved(r):
        wide = jnp.dot(spread[r, :], edge_both[...], preferred_element_type=jnp.float32)
        return wide[:, 0:cases] + wide[:, cases : 2 * cases]

    def neighbour(d):
        axis, side = d // 2, d % 2
        stride = (sizes[1] * sizes[2], sizes[2], 1)[axis]
        step = (grid.c[axis] + (1 if side else -1) + sizes[axis]) % sizes[axis] - grid.c[axis]
        return me + step * stride

    to_scalars = pltpu.make_async_copy(map_all, all_map, load_sem.at[6])
    gathers = []
    for iteration in range(ITERS):
        turn = 0
        slot = iteration % term_all.shape[0]
        if iteration:
            with jax.named_scope("splitx"):
                split_beside(solution, both)
            with jax.named_scope("stiff"):
                by_rows(unknowns, 256, stiff)
            with jax.named_scope("xstart"):
                for old in (0, 1):
                    exchange_drain(old)
                for gather in gathers:
                    gather.drain()
                gathers = []
                exchange_start(turn, field)
        else:
            load_l.wait()

        def before(r):
            value = loads[r, :] - field[r, :]
            field[r, :] = value
            h, l = split(value)
            both[r, 0:cases] = h
            both[r, cases : 2 * cases] = l

        with jax.named_scope("before"):
            by_rows(unknowns, 128, before)
            early[...] = product(t_high[...], t_low[...], both)
        with jax.named_scope("xwait"):
            exchange_wait(turn)
        with jax.named_scope("term"):
            split_beside(arrived[turn], edge_both)
            mine = pl.multiple_of(me * primal, primal)
            term_all[slot, pl.ds(mine, primal), :] = early[...] - product(p_high[...], p_low[...], edge_both)
        terms = Halves(grid, term_all.at[slot], primal, term_send, term_recv)
        with jax.named_scope("termstart"):
            terms.start()
        gathers.append(terms)

        def settle(r):
            value = field[r, :] - moved(r)
            residual[r, :] = value
            h, l = split(weight[r, :] * value)
            both[r, 0:cases] = h
            both[r, cases : 2 * cases] = l

        if iteration == 0:
            with jax.named_scope("spread"):
                slot_rows[...] = jnp.full(slot_rows.shape, -1, jnp.int32)
                for d in range(6):
                    slot_rows[:, d * face : (d + 1) * face] = slot_lists[d]
                hits = slot_rows[...]
                tile = tile_of(unknowns, 64)

                def mark(i, carry):
                    r = pl.ds(pl.multiple_of(i * tile, tile), tile)
                    row = lax.broadcasted_iota(jnp.int32, (tile, edge), 0) + i * tile
                    spread[r, :] = jnp.where(row == hits, 1.0, 0.0).astype(jnp.bfloat16)
                    return carry

                lax.fori_loop(0, unknowns // tile, mark, 0)
                corrected[...] = jnp.zeros_like(corrected)
        with jax.named_scope("settle"):
            by_rows(unknowns, 256, settle)
        if iteration == ITERS - 1:
            out_residual = pltpu.make_async_copy(residual, residual_out, out_sem.at[0])
            out_residual.start()

        def invert(r):
            local[r, :] = weight[r, :] * product(b_high[r, :], b_low[r, :], both)

        def inverts(i):
            def run():
                with jax.named_scope("invert"):
                    invert(pl.ds(i * chunk, chunk))

            return run

        def splits(i):
            def run():
                with jax.named_scope("splitb"):
                    if i == 0:
                        load_b.wait()
                    r = pl.ds(i * chunk, chunk)
                    split_rows(full.at[r], b_high.at[r], b_low.at[r])

            return run

        def turn_coarse():
            with jax.named_scope("transc"):
                load_c.wait()
                for k in range(0, coarse_own.shape[1], 128):
                    coarse_t[k : k + 128, :] = coarse_own[:, k : k + 128].T

        def read_maps():
            with jax.named_scope("maps"):
                if grid.count > 1:
                    block = map_all.at[pl.ds(0, grid.count - 1)]
                    pltpu.make_async_remote_copy(
                        src_ref=block, dst_ref=block, send_sem=map_send, recv_sem=map_recv,
                        device_id=grid.c, device_id_type=MESH,
                    ).wait()
                to_scalars.start()

        def pick(p, carry):
            take_rows(picked, coarse_t, all_map.at[p, 0], primal)
            h, l = split(picked[...].T)
            k = pl.ds(pl.multiple_of(p * primal, primal), primal)
            c_high[:, k] = h
            c_low[:, k] = l
            return carry

        plane = grid.count // sizes[0]
        width = plane * primal
        coarse_tile = term_both.shape[0]
        mine = pl.multiple_of(me * own, own)
        sol_all[iteration][pl.ds(mine, own), :] = jnp.zeros((own, cases), jnp.float32)

        def plane_of(head):
            return (grid.c[0] + sizes[0] - head) % sizes[0]

        def picks(head, part, parts):
            def run():
                with jax.named_scope("pick"):
                    if head == 0 and part == 0:
                        to_scalars.wait()
                    first = plane_of(head) * plane
                    lax.fori_loop(first + plane * part // parts, first + plane * (part + 1) // parts, pick, 0)

            return run

        def collects(d):
            def run():
                with jax.named_scope("clocal"):
                    collect(1, local, d)

            return run

        if iteration == 0:
            read_maps()
            first = [turn_coarse] + [picks(head, part, 4) for head in range(sizes[0]) for part in range(4)]
            work = [splits(i) for i in range(chunks)]
        else:
            first, work = [], []
        work += [inverts(i) for i in range(chunks)] + [collects(d) for d in range(6)]

        def after_plane(head):
            def coarse(i, carry):
                k = pl.ds(pl.multiple_of(plane_of(head) * width + i * coarse_tile, coarse_tile), coarse_tile)
                split_beside(term_all.at[slot, k], term_both)
                sol_all[iteration][pl.ds(mine, own), :] += product(c_high[:, k], c_low[:, k], term_both)
                return carry

            with jax.named_scope("coarse"):
                lax.fori_loop(0, width // coarse_tile, coarse, 0)

        with jax.named_scope("termfin"):
            terms.finish(first, work, after_plane)
        sols = Halves(grid, sol_all[iteration], own, sol_send, sol_recv)
        with jax.named_scope("solstart"):
            sols.start()
        gathers.append(sols)

        with jax.named_scope("xlocal"):
            for d in range(6):
                dispatch(1, d)

        def approach(r):
            solution[r, :] = solution[r, :] + damping * (local[r, :] + moved(r))

        def approaches(i):
            def run():
                with jax.named_scope("approach"):
                    if i == 0:
                        exchange_wait(1)
                        split_beside(arrived[1], edge_both)
                    approach(pl.ds(i * chunk, chunk))

            return run

        def shapes():
            with jax.named_scope("shapes"):
                exchange_wait(shape_turn)
                split_rows(arrived[shape_turn], n_high, n_low)

        nothing = [lambda: None] * (2 * (sum(grid.stages[:1]) - 1))
        work = ([shapes] if iteration == 0 else []) + nothing + [approaches(i) for i in range(chunks)]
        with jax.named_scope("solfin"):
            sols.finish((), work)
        with jax.named_scope("take"):
            take_rows(coarse_rows, sol_all[iteration], all_map.at[me, 0], primal)
            split_beside(coarse_rows, sol_both)
            for d in range(6):

                @pl.when(exists(d))
                def _():
                    q = neighbour(d)
                    r = slice(d * face, (d + 1) * face)
                    take_rows(coarse_rows, sol_all[iteration], all_map.at[q, 0], primal)
                    split_beside(coarse_rows, term_both.at[0:primal])
                    corrected[r, :] = product(n_high[r, :], n_low[r, :], term_both.at[0:primal])

            split_beside(corrected, edge_both)

        def advance(r):
            change = product(m_high[r, :], m_low[r, :], sol_both) + moved(r)
            solution[r, :] = solution[r, :] + damping * change

        with jax.named_scope("advance"):
            by_rows(unknowns, 256, advance)
    with jax.named_scope("out"):
        out_solution = pltpu.make_async_copy(solution, solution_out, out_sem.at[1])
        out_solution.start()
        for turn in range(3):
            exchange_drain(turn)
        for gather in gathers:
            gather.drain()
        out_residual.wait()
        out_solution.wait()


def body(sizes, loads, start, schur, inv_local, basis, coarse_inv, face_index, multiplicity, primal_map):
    unknowns, cases = loads.shape[3:]
    face = face_index.shape[4]
    primal = basis.shape[4]
    count = sizes[0] * sizes[1] * sizes[2]
    total = coarse_inv.shape[1]
    own = coarse_inv.shape[0] // sizes[2]
    edge = -(-6 * face // 128) * 128
    anywhere = pl.BlockSpec(memory_space=pl.ANY)
    dma = pltpu.SemaphoreType.DMA
    f32, bf16 = jnp.float32, jnp.bfloat16
    turns = 3
    coarse_tile = tile_of(count // sizes[0] * primal, 1024)
    grid_stages = stages_of(sizes)
    landings = max(arrivals(grid_stages), arrivals((grid_stages[0], grid_stages[2], grid_stages[1], grid_stages[3])))
    term_slots = ITERS if ITERS * count * primal <= 8 * unknowns else 1
    vec = pltpu.VMEM((unknowns, cases), f32)
    out = jax.ShapeDtypeStruct((unknowns, cases), f32)
    lists = face_index.reshape(6, 1, face)
    solution, residual = pl.pallas_call(
        functools.partial(main_kernel, sizes, face),
        out_shape=(out, out),
        in_specs=[anywhere] * 9,
        out_specs=(anywhere, anywhere),
        scratch_shapes=[
            pltpu.SMEM((6, 1, face), jnp.int32),
            pltpu.VMEM((6, 1, face), jnp.int32),
            pltpu.VMEM((1, unknowns), jnp.int32),
            pltpu.VMEM((unknowns, unknowns), f32),
            pltpu.VMEM((unknowns, unknowns), bf16),
            pltpu.VMEM((unknowns, unknowns), bf16),
            pltpu.VMEM((unknowns, unknowns), bf16),
            pltpu.VMEM((unknowns, unknowns), bf16),
            pltpu.VMEM((unknowns, primal), bf16),
            pltpu.VMEM((unknowns, primal), bf16),
            pltpu.VMEM((primal, unknowns), bf16),
            pltpu.VMEM((primal, unknowns), bf16),
            pltpu.VMEM((primal, edge), bf16),
            pltpu.VMEM((primal, edge), bf16),
            pltpu.VMEM((edge, primal), bf16),
            pltpu.VMEM((edge, primal), bf16),
            pltpu.VMEM((own, count * primal), bf16),
            pltpu.VMEM((own, count * primal), bf16),
            pltpu.VMEM((own, total), f32),
            pltpu.VMEM((total, own), f32),
            pltpu.VMEM((count, 1, primal), jnp.int32),
            pltpu.SMEM((count, 1, primal), jnp.int32),
            pltpu.VMEM((primal, own), f32),
            pltpu.VMEM((1, edge), jnp.int32),
            pltpu.VMEM((unknowns, edge), bf16),
            vec, vec, pltpu.VMEM((unknowns, primal), f32), vec, vec, vec, vec,
            pltpu.VMEM((primal, cases), f32),
            pltpu.VMEM((unknowns, 2 * cases), bf16),
            pltpu.VMEM((edge, 2 * cases), bf16),
            pltpu.VMEM((coarse_tile, 2 * cases), bf16),
            pltpu.VMEM((primal, 2 * cases), bf16),
            pltpu.VMEM((primal, cases), f32),
            pltpu.VMEM((edge, cases), f32),
            pltpu.VMEM((turns, edge, cases), f32),
            [pltpu.VMEM((edge, cases), f32) for _ in range(turns)],
            pltpu.VMEM((term_slots, count * primal, cases), f32),
            [pltpu.VMEM((total, cases), f32) for _ in range(ITERS)],
            dma((11 + unknowns // tile_of(unknowns, 256),)), dma((2,)),
            dma(()), dma(()),
            dma((turns, 6)), dma((turns, 6)),
            dma((2,)), dma((2, landings)),
            dma((2,)), dma((2, landings)),
        ],
        compiler_params=pltpu.CompilerParams(
            collective_id=1, has_side_effects=True, vmem_limit_bytes=67043328
        ),
    )(
        lists, multiplicity.reshape(1, unknowns), primal_map.reshape(1, primal),
        loads.reshape(unknowns, cases), start.reshape(unknowns, cases), basis.reshape(unknowns, primal),
        schur.reshape(unknowns, unknowns), inv_local.reshape(unknowns, unknowns), coarse_inv,
    )
    return (solution.reshape(loads.shape), residual.reshape(loads.shape))


def solution(mesh):
    sizes = tuple(mesh.shape[a] for a in AXES)
    field = P("gx", "gy", "gz", None, None)
    placed = (field,) * 5 + (P(("gx", "gy"), None), field, P("gx", "gy", "gz", None), P("gx", "gy", "gz", None))
    return jax.shard_map(
        functools.partial(body, sizes),
        mesh=mesh,
        in_specs=placed,
        out_specs=(field, field),
        check_vma=False,
    )
```

```python
import functools
import itertools

import jax
import jax.numpy as jnp
from jax import lax
from jax.experimental import pallas as pl
from jax.experimental.pallas import tpu as pltpu
from jax.sharding import PartitionSpec as P

ITERS = 2
damping = 0.6
MESH = pl.DeviceIdType.MESH
AXES = ("gx", "gy", "gz")


def stages_of(sizes):
    gx, gy, gz = sizes
    lo = 2 if gz % 2 == 0 else 1
    return (gx, gy, gz // lo, lo)


class Grid:
    def __init__(self, sizes):
        self.sizes = sizes
        gx, gy, gz = sizes
        self.stages = stages_of(sizes)
        self.hi, self.lo = self.stages[2:]
        self.count = gx * gy * gz
        self.c = tuple(lax.axis_index(a) for a in AXES)
        self.place = (self.c[0], self.c[1], self.c[2] // self.lo, self.c[2] % self.lo)
        z = self.c[0]
        if gx == 4:
            inner = (z % 3 + 1) // 2
            self.line = (z, z + 1 - 2 * (z % 2), 2 - z // 2, 3 - 3 * (z // 2))
            self.back = (0, 1, 3 - inner, 3 - inner)
        else:
            self.line = tuple((z + gx - d) % gx for d in range(gx))
            self.back = tuple((gx - d) % gx for d in range(gx))

    def linear(self, place):
        x, y, h, l = place
        return (x * self.sizes[1] + y) * self.sizes[2] + h * self.lo + l

    def device(self, place):
        x, y, h, l = place
        return (x, y, h * self.lo + l)

    def others(self, function):
        along = [[(c + d) % n for d in range(n)] for c, n in zip(self.c, self.sizes)]
        for target in list(itertools.product(*along))[1:]:
            function(target)

    def announce(self):
        semaphore = pltpu.get_barrier_semaphore()
        self.others(
            lambda target: pl.semaphore_signal(
                semaphore, inc=1, device_id=target, device_id_type=MESH
            )
        )

    def meet(self):
        if self.count > 1:
            pl.semaphore_wait(pltpu.get_barrier_semaphore(), self.count - 1)


class Gather:
    def __init__(self, grid, buffer, whole, band, order, send, recv):
        self.grid, self.buffer, self.whole, self.band = grid, buffer, whole, band
        self.order, self.send, self.recv = order, send, recv
        self.lengths = tuple(grid.stages[o] for o in order)

    def place(self, offset):
        g = self.grid
        place = list(g.place)
        for o, d in zip(self.order, offset):
            if o == 0:
                place[0] = g.line[d]
            elif d:
                place[o] = (g.place[o] + g.stages[o] - d) % g.stages[o]
        return place

    def block(self, offset):
        first = self.grid.linear(self.place(offset)) * self.whole + self.band[0]
        return self.buffer.at[pl.ds(pl.multiple_of(first, 8), self.band[1])]

    def number(self, offset):
        if offset[3]:
            return arrivals(self.lengths) - self.lengths[0] + offset[0]
        value = 0
        for d, n in zip(offset[:3], self.lengths[:3]):
            value = value * n + d
        return value - 1

    def copy(self, block, k, target):
        return pltpu.make_async_remote_copy(
            src_ref=block, dst_ref=block, send_sem=self.send, recv_sem=self.recv.at[k],
            device_id=target, device_id_type=MESH,
        )

    def forward(self, offset, first):
        for stage in range(first, 4):
            for delta in range(1, self.lengths[stage]):
                back = [0, 0, 0, 0]
                back[stage] = delta
                arrived = list(offset)
                axis = self.order[stage]
                arrived[stage] = self.grid.back[delta] if axis == 0 else self.lengths[stage] - delta
                self.copy(
                    self.block(offset), self.number(arrived), self.grid.device(self.place(back))
                ).start()

    def start(self):
        self.forward((0, 0, 0, 0), 0)

    def finish(self, stage, head, idle=None):
        for rest in itertools.product(*[range(n) for n in self.lengths[:stage]]):
            for delta in range(1, self.lengths[stage]):
                arrived = tuple(rest) + (delta,) + (0,) * (3 - stage)
                if arrived[0] != head:
                    continue
                self.copy(self.block(arrived), self.number(arrived), self.grid.c).wait_recv()
                self.forward(arrived, stage + 1)
                if idle:
                    idle()

    def close(self, head):
        n = self.lengths
        rows = n[1] * n[2] * (n[3] - 1) * self.band[1]
        if rows:
            block = self.buffer.at[pl.ds(0, rows)]
            self.copy(block, self.number((head, 0, 0, 1)), self.grid.c).wait_recv()

    def drain(self):
        if self.grid.count > 1:
            block = self.buffer.at[pl.ds(0, (self.grid.count - 1) * self.band[1])]
            self.copy(block, 0, self.grid.c).wait_send()


def arrivals(lengths):
    return lengths[0] * lengths[1] * lengths[2] - 1 + lengths[0]


class Halves:
    def __init__(self, grid, buffer, rows, send, recv):
        half = rows // 2
        self.heads = grid.stages[0]
        self.parts = [
            Gather(grid, buffer, rows, (i * half, half), order, send.at[i], recv.at[i])
            for i, order in enumerate(((0, 1, 2, 3), (0, 2, 1, 3)))
        ]

    def start(self):
        for part in self.parts:
            part.start()

    def waits(self, stages):
        total = 0
        for part in self.parts:
            ahead = 1
            for n in part.lengths[:stages]:
                total += ahead * (n - 1)
                ahead *= n
        return total

    def finish(self, first=(), work=(), after=None):
        first, work = list(first), list(work)

        def idle():
            if first or work:
                (first or work).pop(0)()

        for stage in range(2):
            for head in range(self.heads):
                for part in self.parts:
                    part.finish(stage, head, idle)

        def close(head):
            for part in self.parts:
                part.close(head)
            while first:
                idle()
            if after:
                after(head)

        for head in range(self.heads):
            for part in self.parts:
                part.finish(2, head, idle)
            if head:
                close(head - 1)
        while first or work:
            idle()
        close(self.heads - 1)

    def drain(self):
        for part in self.parts:
            part.drain()


def split(value):
    high = value.astype(jnp.bfloat16)
    low = (value - high.astype(jnp.float32)).astype(jnp.bfloat16)
    return high, low


def tile_of(total, want):
    while total % want:
        want //= 2
    return want


def split_rows(source, high, low):
    rows = source.shape[0]
    tile = tile_of(rows, 64)

    def step(i, carry):
        r = pl.ds(pl.multiple_of(i * tile, tile), tile)
        h, l = split(source[r, :])
        high[r, :] = h
        low[r, :] = l
        return carry

    lax.fori_loop(0, rows // tile, step, 0)


def split_beside(source, both):
    rows, width = source.shape
    tile = tile_of(rows, 128)

    def step(i, carry):
        r = pl.ds(pl.multiple_of(i * tile, tile), tile)
        h, l = split(source[r, :])
        both[r, 0:width] = h
        both[r, width : 2 * width] = l
        return carry

    lax.fori_loop(0, rows // tile, step, 0)


def product(high, low, both):
    width = both.shape[1] // 2
    wide = jnp.dot(high, both[...], preferred_element_type=jnp.float32)
    thin = jnp.dot(low, both[:, 0:width], preferred_element_type=jnp.float32)
    return wide[:, 0:width] + wide[:, width:] + thin


def by_rows(rows, want, function):
    tile = tile_of(rows, want)

    def step(i, carry):
        function(pl.ds(pl.multiple_of(i * tile, tile), tile))
        return carry

    lax.fori_loop(0, rows // tile, step, 0)


def take_rows(target, source, index, count):
    unroll = tile_of(count, 32)

    def step(i, carry):
        first = pl.multiple_of(i * unroll, unroll)
        for j in range(unroll):
            target[pl.ds(first + j, 1), :] = source[pl.ds(index[first + j], 1), :]
        return carry

    lax.fori_loop(0, count // unroll, step, 0)


def pause():
    pass


def main_kernel(
    sizes, face,
    lists_in, multiplicity_in, own_map_in,
    loads_in, start_in, basis_in, schur, inverse, coarse_inv,
    solution_out, residual_out,
    slots, slot_lists, multiplicity, full, s_high, s_low, b_high, b_low, m_high, m_low, t_high, t_low, p_high, p_low, n_high, n_low,
    c_high, c_low, coarse_own, coarse_t, map_all, all_map, picked, slot_rows, spread,
    loads, solution, basis, weight, residual, field, local, early, both, edge_both, term_both, sol_both, coarse_rows, corrected,
    faces, arrived, term_all, sol_all,
    load_sem, out_sem, map_send, map_recv, face_send, face_recv, term_send, term_recv, sol_send, sol_recv,
):
    grid = Grid(sizes)
    unknowns, cases = solution.shape
    primal = basis.shape[1]
    own = coarse_t.shape[1]
    edge = corrected.shape[0]
    shape_turn = 2
    first_own = pl.multiple_of(grid.c[2] * own, own)

    def load(k, source, target):
        return pltpu.make_async_copy(source, target, load_sem.at[k])

    load_x = load(0, start_in, solution)
    chunk = tile_of(unknowns, 256)
    chunks = unknowns // chunk
    load_s = [
        load(7 + i, schur.at[pl.ds(i * chunk, chunk)], full.at[pl.ds(i * chunk, chunk)]) for i in range(chunks)
    ]
    load_m = load(2, basis_in, basis)
    load_l = load(3, loads_in, loads)
    load_c = load(4, coarse_inv.at[pl.ds(first_own, own)], coarse_own)
    load_b = load(5, inverse, full)
    load_i = [
        load(7 + chunks, lists_in, slots), load(8 + chunks, lists_in, slot_lists),
        load(9 + chunks, multiplicity_in, multiplicity),
    ]
    me = grid.linear(grid.place)
    load_o = load(10 + chunks, own_map_in, map_all.at[me])
    for each in (load_x, *load_s, *load_i, load_o, load_m, load_l, load_c):
        each.start()
    for landing in arrived:
        landing[...] = jnp.zeros_like(landing)
    with jax.named_scope("announce"):
        grid.announce()

    with jax.named_scope("splitx"):
        load_x.wait()
        split_beside(solution, both)

    def stiff(r):
        field[r, :] = product(s_high[r, :], s_low[r, :], both)

    with jax.named_scope("stiff0"):
        for i in range(chunks):
            r = pl.ds(i * chunk, chunk)
            load_s[i].wait()
            split_rows(full.at[r], s_high.at[r], s_low.at[r])
            stiff(r)
    load_b.start()

    def face_copy(turn, d):
        axis, side = d // 2, d % 2
        target = list(grid.c)
        target[axis] = grid.c[axis] + (1 if side else -1)
        return pltpu.make_async_remote_copy(
            src_ref=faces.at[turn, pl.ds(d * face, face)],
            dst_ref=arrived[turn].at[pl.ds((d ^ 1) * face, face)],
            send_sem=face_send.at[turn, d],
            recv_sem=face_recv.at[turn, d ^ 1],
            device_id=tuple(target), device_id_type=MESH,
        )

    def exists(d):
        axis, side = d // 2, d % 2
        return grid.c[axis] < sizes[axis] - 1 if side else grid.c[axis] > 0

    def collect(turn, source, d):
        take_rows(faces.at[turn, pl.ds(d * face, face)], source, slots.at[d, 0], face)

    def dispatch(turn, d):
        @pl.when(exists(d))
        def _():
            face_copy(turn, d).start()

    def exchange_start(turn, source):
        for d in range(6):
            collect(turn, source, d)
            dispatch(turn, d)

    def exchange_wait(turn):
        for d in range(6):

            @pl.when(exists(d))
            def _():
                block = arrived[turn].at[pl.ds(d * face, face)]
                pltpu.make_async_remote_copy(
                    src_ref=block, dst_ref=block, send_sem=face_send.at[turn, d],
                    recv_sem=face_recv.at[turn, d], device_id=grid.c, device_id_type=MESH,
                ).wait_recv()

    def exchange_drain(turn):
        for d in range(6):

            @pl.when(exists(d))
            def _():
                face_copy(turn, d).wait_send()

    with jax.named_scope("collect"):
        for each in (*load_i, load_o):
            each.wait()
        collect(0, field, 0)
    with jax.named_scope("meet"):
        grid.meet()
    with jax.named_scope("xstart"):
        dispatch(0, 0)
        for d in range(1, 6):
            collect(0, field, d)
            dispatch(0, d)
    with jax.named_scope("mapsend"):

        def map_copy(target):
            return pltpu.make_async_remote_copy(
                src_ref=map_all.at[me], dst_ref=map_all.at[me], send_sem=map_send, recv_sem=map_recv,
                device_id=target, device_id_type=MESH,
            )

        grid.others(lambda target: map_copy(target).start())
    with jax.named_scope("basis"):
        load_m.wait()
        for k in range(0, unknowns, 128):
            r = slice(k, k + 128)
            inverse_count = 1.0 / multiplicity[:, r].astype(jnp.float32)
            weight[r, :] = jnp.broadcast_to(inverse_count, (cases, 128)).T
            scaled = weight[r, 0:1] * basis[r, :]
            basis[r, :] = scaled
            h, l = split(scaled)
            m_high[r, :] = h
            m_low[r, :] = l
            h, l = split(scaled.T)
            t_high[:, r] = h
            t_low[:, r] = l
    with jax.named_scope("psi"):
        for d in range(6):
            collect(shape_turn, basis, d)
        shape_edges = faces.at[shape_turn]
        if edge > 6 * face:
            shape_edges[6 * face : edge, :] = jnp.zeros((edge - 6 * face, cases), jnp.float32)
        for k in range(0, edge, 128):
            h, l = split(shape_edges[k : k + 128, :].T)
            p_high[:, k : k + 128] = h
            p_low[:, k : k + 128] = l
    for d in range(6):
        dispatch(shape_turn, d)

    def moved(r):
        wide = jnp.dot(spread[r, :], edge_both[...], preferred_element_type=jnp.float32)
        return wide[:, 0:cases] + wide[:, cases : 2 * cases]

    def neighbour(d):
        axis, side = d // 2, d % 2
        stride = (sizes[1] * sizes[2], sizes[2], 1)[axis]
        step = (grid.c[axis] + (1 if side else -1) + sizes[axis]) % sizes[axis] - grid.c[axis]
        return me + step * stride

    to_scalars = pltpu.make_async_copy(map_all, all_map, load_sem.at[6])
    out_solution = [
        pltpu.make_async_copy(
            solution.at[pl.ds(i * chunk, chunk)], solution_out.at[pl.ds(i * chunk, chunk)], out_sem.at[1 + i]
        )
        for i in range(chunks)
    ]
    gathers = []
    for iteration in range(ITERS):
        turn = 0
        slot = iteration % term_all.shape[0]
        if iteration:
            with jax.named_scope("stiff"):
                by_rows(unknowns, 256, stiff)
            with jax.named_scope("xstart"):
                for old in (0, 1):
                    exchange_drain(old)
                for gather in gathers:
                    gather.drain()
                gathers = []
                exchange_start(turn, field)
        else:
            load_l.wait()

        def before(r):
            value = loads[r, :] - field[r, :]
            field[r, :] = value
            h, l = split(value)
            both[r, 0:cases] = h
            both[r, cases : 2 * cases] = l

        with jax.named_scope("before"):
            by_rows(unknowns, 128, before)
            early[...] = product(t_high[...], t_low[...], both)
        with jax.named_scope("xwait"):
            exchange_wait(turn)
        with jax.named_scope("term"):
            split_beside(arrived[turn], edge_both)
            mine = pl.multiple_of(me * primal, primal)
            term_all[slot, pl.ds(mine, primal), :] = early[...] - product(p_high[...], p_low[...], edge_both)
        terms = Halves(grid, term_all.at[slot], primal, term_send, term_recv)
        with jax.named_scope("termstart"):
            terms.start()
        gathers.append(terms)

        def settle(r):
            value = field[r, :] - moved(r)
            residual[r, :] = value
            h, l = split(weight[r, :] * value)
            both[r, 0:cases] = h
            both[r, cases : 2 * cases] = l

        if iteration == 0:
            with jax.named_scope("spread"):
                slot_rows[...] = jnp.full(slot_rows.shape, -1, jnp.int32)
                for d in range(6):
                    slot_rows[:, d * face : (d + 1) * face] = slot_lists[d]
                hits = slot_rows[...]
                tile = tile_of(unknowns, 64)

                def mark(i, carry):
                    r = pl.ds(pl.multiple_of(i * tile, tile), tile)
                    row = lax.broadcasted_iota(jnp.int32, (tile, edge), 0) + i * tile
                    spread[r, :] = jnp.where(row == hits, 1.0, 0.0).astype(jnp.bfloat16)
                    return carry

                lax.fori_loop(0, unknowns // tile, mark, 0)
                corrected[...] = jnp.zeros_like(corrected)
        with jax.named_scope("settle"):
            by_rows(unknowns, 256, settle)
        if iteration == ITERS - 1:
            out_residual = pltpu.make_async_copy(residual, residual_out, out_sem.at[0])
            out_residual.start()

        def invert(r):
            local[r, :] = weight[r, :] * product(b_high[r, :], b_low[r, :], both)

        def inverts(i):
            def run():
                with jax.named_scope("invert"):
                    invert(pl.ds(i * chunk, chunk))

            return run

        def splits(i):
            def run():
                with jax.named_scope("splitb"):
                    if i == 0:
                        load_b.wait()
                    r = pl.ds(i * chunk, chunk)
                    split_rows(full.at[r], b_high.at[r], b_low.at[r])

            return run

        def turn_coarse():
            with jax.named_scope("transc"):
                load_c.wait()
                for k in range(0, coarse_own.shape[1], 128):
                    coarse_t[k : k + 128, :] = coarse_own[:, k : k + 128].T

        def read_maps():
            with jax.named_scope("maps"):
                if grid.count > 1:
                    block = map_all.at[pl.ds(0, grid.count - 1)]
                    pltpu.make_async_remote_copy(
                        src_ref=block, dst_ref=block, send_sem=map_send, recv_sem=map_recv,
                        device_id=grid.c, device_id_type=MESH,
                    ).wait()
                to_scalars.start()

        def pick(p, carry):
            take_rows(picked, coarse_t, all_map.at[p, 0], primal)
            h, l = split(picked[...].T)
            k = pl.ds(pl.multiple_of(p * primal, primal), primal)
            c_high[:, k] = h
            c_low[:, k] = l
            return carry

        plane = grid.count // sizes[0]
        width = plane * primal
        coarse_tile = term_both.shape[0]
        mine = pl.multiple_of(me * own, own)
        sol_all[iteration][pl.ds(mine, own), :] = jnp.zeros((own, cases), jnp.float32)

        def plane_of(head):
            return grid.line[head]

        def picks(head, part, parts):
            def run():
                with jax.named_scope("pick"):
                    if head == 0 and part == 0:
                        to_scalars.wait()
                    first = plane_of(head) * plane
                    lax.fori_loop(first + plane * part // parts, first + plane * (part + 1) // parts, pick, 0)

            return run

        def collects(d):
            def run():
                with jax.named_scope("clocal"):
                    collect(1, local, d)

            return run

        if iteration == 0:
            read_maps()
            first = [turn_coarse] + [picks(head, part, 4) for head in range(sizes[0]) for part in range(4)]
            work = [splits(i) for i in range(chunks)]
        else:
            first, work = [], []
        def send_local():
            with jax.named_scope("xlocal"):
                for d in range(6):
                    dispatch(1, d)

        work += [inverts(i) for i in range(chunks)] + [collects(d) for d in range(6)]

        def after_plane(head):
            def coarse(i, carry):
                k = pl.ds(pl.multiple_of(plane_of(head) * width + i * coarse_tile, coarse_tile), coarse_tile)
                split_beside(term_all.at[slot, k], term_both)
                sol_all[iteration][pl.ds(mine, own), :] += product(c_high[:, k], c_low[:, k], term_both)
                return carry

            with jax.named_scope("coarse"):
                lax.fori_loop(0, width // coarse_tile, coarse, 0)

        with jax.named_scope("termfin"):
            terms.finish(first, work, after_plane)
        sols = Halves(grid, sol_all[iteration], own, sol_send, sol_recv)
        with jax.named_scope("solstart"):
            sols.start()
        gathers.append(sols)

        send_local()

        def approach(r):
            solution[r, :] = solution[r, :] + damping * (local[r, :] + moved(r))

        def approaches(i):
            def run():
                with jax.named_scope("approach"):
                    if i == 0:
                        exchange_wait(1)
                        split_beside(arrived[1], edge_both)
                    approach(pl.ds(i * chunk, chunk))

            return run

        def shapes():
            with jax.named_scope("shapes"):
                exchange_wait(shape_turn)
                split_rows(arrived[shape_turn], n_high, n_low)

        work = ([shapes] if iteration == 0 else []) + [pause] * sols.waits(1) + [approaches(i) for i in range(chunks)]
        with jax.named_scope("solfin"):
            sols.finish((), work)
        with jax.named_scope("take"):
            take_rows(coarse_rows, sol_all[iteration], all_map.at[me, 0], primal)
            split_beside(coarse_rows, sol_both)
            for d in range(6):

                @pl.when(exists(d))
                def _():
                    q = neighbour(d)
                    r = slice(d * face, (d + 1) * face)
                    take_rows(coarse_rows, sol_all[iteration], all_map.at[q, 0], primal)
                    split_beside(coarse_rows, term_both.at[0:primal])
                    corrected[r, :] = product(n_high[r, :], n_low[r, :], term_both.at[0:primal])

            split_beside(corrected, edge_both)

        def advance(r):
            change = product(m_high[r, :], m_low[r, :], sol_both) + moved(r)
            value = solution[r, :] + damping * change
            solution[r, :] = value
            if iteration < ITERS - 1:
                h, l = split(value)
                both[r, 0:cases] = h
                both[r, cases : 2 * cases] = l

        with jax.named_scope("advance"):
            if iteration < ITERS - 1:
                by_rows(unknowns, 256, advance)
            else:
                for i in range(chunks):
                    r = pl.ds(i * chunk, chunk)
                    advance(r)
                    out_solution[i].start()
    with jax.named_scope("out"):
        for turn in range(3):
            exchange_drain(turn)
        for gather in gathers:
            gather.drain()
        out_residual.wait()
        for each in out_solution:
            each.wait()


def settle_outputs(first_in, second_in, first_out, second_out, stage, come, go):
    pairs = ((first_in, first_out), (second_in, second_out))
    pieces = stage.shape[1]
    rows = stage.shape[2]
    entering, leaving = [], []
    for i in range(pieces):
        for k, (source, target) in enumerate(pairs):
            r = pl.ds(i * rows, rows)
            entering.append(pltpu.make_async_copy(source.at[r], stage.at[k, i], come.at[k, i]))
            leaving.append(pltpu.make_async_copy(stage.at[k, i], target.at[r], go.at[k, i]))
    for each in entering:
        each.start()
    for a, b in zip(entering, leaving):
        a.wait()
        b.start()
    for each in leaving:
        each.wait()


def body(sizes, loads, start, schur, inv_local, basis, coarse_inv, face_index, multiplicity, primal_map):
    unknowns, cases = loads.shape[3:]
    face = face_index.shape[4]
    primal = basis.shape[4]
    count = sizes[0] * sizes[1] * sizes[2]
    total = coarse_inv.shape[1]
    own = coarse_inv.shape[0] // sizes[2]
    edge = -(-6 * face // 128) * 128
    anywhere = pl.BlockSpec(memory_space=pl.ANY)
    dma = pltpu.SemaphoreType.DMA
    f32, bf16 = jnp.float32, jnp.bfloat16
    turns = 3
    coarse_tile = tile_of(count // sizes[0] * primal, 1024)
    grid_stages = stages_of(sizes)
    landings = max(arrivals(grid_stages), arrivals((grid_stages[0], grid_stages[2], grid_stages[1], grid_stages[3])))
    term_slots = ITERS if ITERS * count * primal <= 8 * unknowns else 1
    vec = pltpu.VMEM((unknowns, cases), f32)
    out = jax.ShapeDtypeStruct((unknowns, cases), f32)
    lists = face_index.reshape(6, 1, face)
    solution, residual = pl.pallas_call(
        functools.partial(main_kernel, sizes, face),
        out_shape=(out, out),
        in_specs=[anywhere] * 9,
        out_specs=(anywhere, anywhere),
        scratch_shapes=[
            pltpu.SMEM((6, 1, face), jnp.int32),
            pltpu.VMEM((6, 1, face), jnp.int32),
            pltpu.VMEM((1, unknowns), jnp.int32),
            pltpu.VMEM((unknowns, unknowns), f32),
            pltpu.VMEM((unknowns, unknowns), bf16),
            pltpu.VMEM((unknowns, unknowns), bf16),
            pltpu.VMEM((unknowns, unknowns), bf16),
            pltpu.VMEM((unknowns, unknowns), bf16),
            pltpu.VMEM((unknowns, primal), bf16),
            pltpu.VMEM((unknowns, primal), bf16),
            pltpu.VMEM((primal, unknowns), bf16),
            pltpu.VMEM((primal, unknowns), bf16),
            pltpu.VMEM((primal, edge), bf16),
            pltpu.VMEM((primal, edge), bf16),
            pltpu.VMEM((edge, primal), bf16),
            pltpu.VMEM((edge, primal), bf16),
            pltpu.VMEM((own, count * primal), bf16),
            pltpu.VMEM((own, count * primal), bf16),
            pltpu.VMEM((own, total), f32),
            pltpu.VMEM((total, own), f32),
            pltpu.VMEM((count, 1, primal), jnp.int32),
            pltpu.SMEM((count, 1, primal), jnp.int32),
            pltpu.VMEM((primal, own), f32),
            pltpu.VMEM((1, edge), jnp.int32),
            pltpu.VMEM((unknowns, edge), bf16),
            vec, vec, pltpu.VMEM((unknowns, primal), f32), vec, vec, vec, vec,
            pltpu.VMEM((primal, cases), f32),
            pltpu.VMEM((unknowns, 2 * cases), bf16),
            pltpu.VMEM((edge, 2 * cases), bf16),
            pltpu.VMEM((coarse_tile, 2 * cases), bf16),
            pltpu.VMEM((primal, 2 * cases), bf16),
            pltpu.VMEM((primal, cases), f32),
            pltpu.VMEM((edge, cases), f32),
            pltpu.VMEM((turns, edge, cases), f32),
            [pltpu.VMEM((edge, cases), f32) for _ in range(turns)],
            pltpu.VMEM((term_slots, count * primal, cases), f32),
            [pltpu.VMEM((total, cases), f32) for _ in range(ITERS)],
            dma((11 + unknowns // tile_of(unknowns, 256),)), dma((1 + unknowns // tile_of(unknowns, 256),)),
            dma(()), dma(()),
            dma((turns, 6)), dma((turns, 6)),
            dma((2,)), dma((2, landings)),
            dma((2,)), dma((2, landings)),
        ],
        compiler_params=pltpu.CompilerParams(
            collective_id=1, has_side_effects=True, vmem_limit_bytes=67043328
        ),
    )(
        lists, multiplicity.reshape(1, unknowns), primal_map.reshape(1, primal),
        loads.reshape(unknowns, cases), start.reshape(unknowns, cases), basis.reshape(unknowns, primal),
        schur.reshape(unknowns, unknowns), inv_local.reshape(unknowns, unknowns), coarse_inv,
    )
    pieces = 2
    rows = unknowns // pieces
    solution, residual = pl.pallas_call(
        settle_outputs,
        out_shape=(out, out),
        in_specs=[anywhere] * 2,
        out_specs=(anywhere, anywhere),
        scratch_shapes=[pltpu.VMEM((2, pieces, rows, cases), f32), dma((2, pieces)), dma((2, pieces))],
    )(solution, residual)
    return (solution.reshape(loads.shape), residual.reshape(loads.shape))


def solution(mesh):
    sizes = tuple(mesh.shape[a] for a in AXES)
    field = P("gx", "gy", "gz", None, None)
    placed = (field,) * 5 + (P(("gx", "gy"), None), field, P("gx", "gy", "gz", None), P("gx", "gy", "gz", None))
    return jax.shard_map(
        functools.partial(body, sizes),
        mesh=mesh,
        in_specs=placed,
        out_specs=(field, field),
        check_vma=False,
    )
```

```python
import functools
import itertools

import jax
import jax.numpy as jnp
from jax import lax
from jax.experimental import pallas as pl
from jax.experimental.pallas import tpu as pltpu
from jax.sharding import PartitionSpec as P

ITERS = 2
damping = 0.6
MESH = pl.DeviceIdType.MESH
AXES = ("gx", "gy", "gz")


def stages_of(sizes):
    gx, gy, gz = sizes
    lo = 2 if gz % 2 == 0 else 1
    return (gx, gy, gz // lo, lo)


class Grid:
    def __init__(self, sizes):
        self.sizes = sizes
        gx, gy, gz = sizes
        self.stages = stages_of(sizes)
        self.hi, self.lo = self.stages[2:]
        self.count = gx * gy * gz
        self.c = tuple(lax.axis_index(a) for a in AXES)
        self.place = (self.c[0], self.c[1], self.c[2] // self.lo, self.c[2] % self.lo)
        z = self.c[0]
        if gx == 4:
            inner = (z % 3 + 1) // 2
            self.line = (z, z + 1 - 2 * (z % 2), 2 - z // 2, 3 - 3 * (z // 2))
            self.back = (0, 1, 3 - inner, 3 - inner)
        else:
            self.line = tuple((z + gx - d) % gx for d in range(gx))
            self.back = tuple((gx - d) % gx for d in range(gx))

    def linear(self, place):
        x, y, h, l = place
        return (x * self.sizes[1] + y) * self.sizes[2] + h * self.lo + l

    def device(self, place):
        x, y, h, l = place
        return (x, y, h * self.lo + l)

    def others(self, function):
        along = [[(c + d) % n for d in range(n)] for c, n in zip(self.c, self.sizes)]
        for target in list(itertools.product(*along))[1:]:
            function(target)

    def announce(self):
        semaphore = pltpu.get_barrier_semaphore()
        self.others(
            lambda target: pl.semaphore_signal(
                semaphore, inc=1, device_id=target, device_id_type=MESH
            )
        )

    def meet(self):
        if self.count > 1:
            pl.semaphore_wait(pltpu.get_barrier_semaphore(), self.count - 1)


class Gather:
    def __init__(self, grid, buffer, whole, band, order, send, recv):
        self.grid, self.buffer, self.whole, self.band = grid, buffer, whole, band
        self.order, self.send, self.recv = order, send, recv
        self.lengths = tuple(grid.stages[o] for o in order)

    def place(self, offset):
        g = self.grid
        place = list(g.place)
        for o, d in zip(self.order, offset):
            if o == 0:
                place[0] = g.line[d]
            elif d:
                place[o] = (g.place[o] + g.stages[o] - d) % g.stages[o]
        return place

    def block(self, offset):
        first = self.grid.linear(self.place(offset)) * self.whole + self.band[0]
        return self.buffer.at[pl.ds(pl.multiple_of(first, 8), self.band[1])]

    def number(self, offset):
        if offset[3]:
            return arrivals(self.lengths) - self.lengths[0] + offset[0]
        value = 0
        for d, n in zip(offset[:3], self.lengths[:3]):
            value = value * n + d
        return value - 1

    def copy(self, block, k, target):
        return pltpu.make_async_remote_copy(
            src_ref=block, dst_ref=block, send_sem=self.send, recv_sem=self.recv.at[k],
            device_id=target, device_id_type=MESH,
        )

    def forward(self, offset, first):
        for stage in range(first, 4):
            for delta in range(1, self.lengths[stage]):
                back = [0, 0, 0, 0]
                back[stage] = delta
                arrived = list(offset)
                axis = self.order[stage]
                arrived[stage] = self.grid.back[delta] if axis == 0 else self.lengths[stage] - delta
                self.copy(
                    self.block(offset), self.number(arrived), self.grid.device(self.place(back))
                ).start()

    def start(self):
        self.forward((0, 0, 0, 0), 0)

    def finish(self, stage, head, idle=None):
        for rest in itertools.product(*[range(n) for n in self.lengths[:stage]]):
            for delta in range(1, self.lengths[stage]):
                arrived = tuple(rest) + (delta,) + (0,) * (3 - stage)
                if arrived[0] != head:
                    continue
                self.copy(self.block(arrived), self.number(arrived), self.grid.c).wait_recv()
                self.forward(arrived, stage + 1)
                if idle:
                    idle()

    def close(self, head):
        n = self.lengths
        rows = n[1] * n[2] * (n[3] - 1) * self.band[1]
        if rows:
            block = self.buffer.at[pl.ds(0, rows)]
            self.copy(block, self.number((head, 0, 0, 1)), self.grid.c).wait_recv()

    def drain(self):
        if self.grid.count > 1:
            block = self.buffer.at[pl.ds(0, (self.grid.count - 1) * self.band[1])]
            self.copy(block, 0, self.grid.c).wait_send()


def arrivals(lengths):
    return lengths[0] * lengths[1] * lengths[2] - 1 + lengths[0]


class Halves:
    def __init__(self, grid, buffer, rows, send, recv):
        half = rows // 2
        self.heads = grid.stages[0]
        self.parts = [
            Gather(grid, buffer, rows, (i * half, half), order, send.at[i], recv.at[i])
            for i, order in enumerate(((0, 1, 2, 3), (0, 2, 1, 3)))
        ]

    def start(self):
        for part in self.parts:
            part.start()

    def waits(self, stages):
        total = 0
        for part in self.parts:
            ahead = 1
            for n in part.lengths[:stages]:
                total += ahead * (n - 1)
                ahead *= n
        return total

    def finish(self, first=(), work=(), after=None):
        first, work = list(first), list(work)

        def idle():
            if first or work:
                (first or work).pop(0)()

        for stage in range(2):
            for head in range(self.heads):
                for part in self.parts:
                    part.finish(stage, head, idle)

        def close(head):
            for part in self.parts:
                part.close(head)
            while first:
                idle()
            if after:
                after(head)

        for head in range(self.heads):
            for part in self.parts:
                part.finish(2, head, idle)
            if head:
                close(head - 1)
        while first or work:
            idle()
        close(self.heads - 1)

    def drain(self):
        for part in self.parts:
            part.drain()


def split(value):
    high = value.astype(jnp.bfloat16)
    low = (value - high.astype(jnp.float32)).astype(jnp.bfloat16)
    return high, low


def tile_of(total, want):
    while total % want:
        want //= 2
    return want


def split_rows(source, high, low):
    rows = source.shape[0]
    tile = tile_of(rows, 64)

    def step(i, carry):
        r = pl.ds(pl.multiple_of(i * tile, tile), tile)
        h, l = split(source[r, :])
        high[r, :] = h
        low[r, :] = l
        return carry

    lax.fori_loop(0, rows // tile, step, 0)


def split_beside(source, both):
    rows, width = source.shape
    tile = tile_of(rows, 128)

    def step(i, carry):
        r = pl.ds(pl.multiple_of(i * tile, tile), tile)
        h, l = split(source[r, :])
        both[r, 0:width] = h
        both[r, width : 2 * width] = l
        return carry

    lax.fori_loop(0, rows // tile, step, 0)


def product(high, low, both):
    width = both.shape[1] // 2
    wide = jnp.dot(high, both[...], preferred_element_type=jnp.float32)
    thin = jnp.dot(low, both[:, 0:width], preferred_element_type=jnp.float32)
    return wide[:, 0:width] + wide[:, width:] + thin


def by_rows(rows, want, function):
    tile = tile_of(rows, want)

    def step(i, carry):
        function(pl.ds(pl.multiple_of(i * tile, tile), tile))
        return carry

    lax.fori_loop(0, rows // tile, step, 0)


def take_rows(target, source, index, count):
    unroll = tile_of(count, 64)

    def step(i, carry):
        first = pl.multiple_of(i * unroll, unroll)
        for j in range(unroll):
            target[pl.ds(first + j, 1), :] = source[pl.ds(index[first + j], 1), :]
        return carry

    lax.fori_loop(0, count // unroll, step, 0)


def pause():
    pass


def main_kernel(
    sizes, face,
    lists_in, multiplicity_in, own_map_in,
    loads_in, start_in, basis_in, schur, inverse, coarse_inv,
    solution_out, residual_out,
    slots, slot_lists, multiplicity, full, s_high, s_low, b_high, b_low, m_high, m_low, t_high, t_low, p_high, p_low, n_high, n_low,
    c_high, c_low, coarse_own, coarse_t, map_all, all_map, picked, slot_rows, spread,
    loads, solution, basis, weight, residual, field, local, early, both, edge_both, term_both, sol_both, coarse_rows, corrected,
    faces, arrived, term_all, sol_all,
    load_sem, out_sem, map_send, map_recv, face_send, face_recv, term_send, term_recv, sol_send, sol_recv,
):
    grid = Grid(sizes)
    unknowns, cases = solution.shape
    primal = basis.shape[1]
    own = coarse_t.shape[1]
    edge = corrected.shape[0]
    shape_turn = 2
    first_own = pl.multiple_of(grid.c[2] * own, own)

    def load(k, source, target):
        return pltpu.make_async_copy(source, target, load_sem.at[k])

    load_x = load(0, start_in, solution)
    chunk = tile_of(unknowns, 256)
    chunks = unknowns // chunk
    load_s = [
        load(7 + i, schur.at[pl.ds(i * chunk, chunk)], full.at[pl.ds(i * chunk, chunk)]) for i in range(chunks)
    ]
    load_m = load(2, basis_in, basis)
    load_l = load(3, loads_in, loads)
    load_c = load(4, coarse_inv.at[pl.ds(first_own, own)], coarse_own)
    load_b = load(5, inverse, full)
    load_i = [
        load(7 + chunks, lists_in, slots), load(8 + chunks, lists_in, slot_lists),
        load(9 + chunks, multiplicity_in, multiplicity),
    ]
    me = grid.linear(grid.place)
    load_o = load(10 + chunks, own_map_in, map_all.at[me])
    for each in (load_x, *load_s, *load_i, load_o, load_m, load_l, load_c):
        each.start()
    for landing in arrived:
        landing[...] = jnp.zeros_like(landing)
    with jax.named_scope("announce"):
        grid.announce()

    with jax.named_scope("splitx"):
        load_x.wait()
        split_beside(solution, both)

    def stiff(r):
        field[r, :] = product(s_high[r, :], s_low[r, :], both)

    with jax.named_scope("stiff0"):
        for i in range(chunks):
            r = pl.ds(i * chunk, chunk)
            load_s[i].wait()
            split_rows(full.at[r], s_high.at[r], s_low.at[r])
            stiff(r)
    load_b.start()

    def face_copy(turn, d):
        axis, side = d // 2, d % 2
        target = list(grid.c)
        target[axis] = grid.c[axis] + (1 if side else -1)
        return pltpu.make_async_remote_copy(
            src_ref=faces.at[turn, pl.ds(d * face, face)],
            dst_ref=arrived[turn].at[pl.ds((d ^ 1) * face, face)],
            send_sem=face_send.at[turn, d],
            recv_sem=face_recv.at[turn, d ^ 1],
            device_id=tuple(target), device_id_type=MESH,
        )

    def exists(d):
        axis, side = d // 2, d % 2
        return grid.c[axis] < sizes[axis] - 1 if side else grid.c[axis] > 0

    def collect(turn, source, d):
        take_rows(faces.at[turn, pl.ds(d * face, face)], source, slots.at[d, 0], face)

    def dispatch(turn, d):
        @pl.when(exists(d))
        def _():
            face_copy(turn, d).start()

    def exchange_start(turn, source):
        for d in range(6):
            collect(turn, source, d)
            dispatch(turn, d)

    def exchange_wait(turn):
        for d in range(6):

            @pl.when(exists(d))
            def _():
                block = arrived[turn].at[pl.ds(d * face, face)]
                pltpu.make_async_remote_copy(
                    src_ref=block, dst_ref=block, send_sem=face_send.at[turn, d],
                    recv_sem=face_recv.at[turn, d], device_id=grid.c, device_id_type=MESH,
                ).wait_recv()

    def exchange_drain(turn):
        for d in range(6):

            @pl.when(exists(d))
            def _():
                face_copy(turn, d).wait_send()

    with jax.named_scope("collect"):
        for each in (*load_i, load_o):
            each.wait()
        collect(0, field, 0)
    with jax.named_scope("meet"):
        grid.meet()
    with jax.named_scope("xstart"):
        dispatch(0, 0)
        for d in range(1, 6):
            collect(0, field, d)
            dispatch(0, d)
    with jax.named_scope("mapsend"):

        def map_copy(target):
            return pltpu.make_async_remote_copy(
                src_ref=map_all.at[me], dst_ref=map_all.at[me], send_sem=map_send, recv_sem=map_recv,
                device_id=target, device_id_type=MESH,
            )

        grid.others(lambda target: map_copy(target).start())
    with jax.named_scope("basis"):
        load_m.wait()
        for k in range(0, unknowns, 128):
            r = slice(k, k + 128)
            inverse_count = 1.0 / multiplicity[:, r].astype(jnp.float32)
            weight[r, :] = jnp.broadcast_to(inverse_count, (cases, 128)).T
            scaled = weight[r, 0:1] * basis[r, :]
            basis[r, :] = scaled
            h, l = split(scaled)
            m_high[r, :] = h
            m_low[r, :] = l
            h, l = split(scaled.T)
            t_high[:, r] = h
            t_low[:, r] = l
    with jax.named_scope("psi"):
        for d in range(6):
            collect(shape_turn, basis, d)
        shape_edges = faces.at[shape_turn]
        if edge > 6 * face:
            shape_edges[6 * face : edge, :] = jnp.zeros((edge - 6 * face, cases), jnp.float32)
        for k in range(0, edge, 128):
            h, l = split(shape_edges[k : k + 128, :].T)
            p_high[:, k : k + 128] = h
            p_low[:, k : k + 128] = l
    for d in range(6):
        dispatch(shape_turn, d)

    def moved(r):
        wide = jnp.dot(spread[r, :], edge_both[...], preferred_element_type=jnp.float32)
        return wide[:, 0:cases] + wide[:, cases : 2 * cases]

    def neighbour(d):
        axis, side = d // 2, d % 2
        stride = (sizes[1] * sizes[2], sizes[2], 1)[axis]
        step = (grid.c[axis] + (1 if side else -1) + sizes[axis]) % sizes[axis] - grid.c[axis]
        return me + step * stride

    to_scalars = pltpu.make_async_copy(map_all, all_map, load_sem.at[6])
    out_solution = [
        pltpu.make_async_copy(
            solution.at[pl.ds(i * chunk, chunk)], solution_out.at[pl.ds(i * chunk, chunk)], out_sem.at[1 + i]
        )
        for i in range(chunks)
    ]
    gathers = []
    for iteration in range(ITERS):
        turn = 0
        slot = iteration % term_all.shape[0]
        if iteration:
            with jax.named_scope("stiff"):
                by_rows(unknowns, 512, stiff)
            with jax.named_scope("xstart"):
                for old in (0, 1):
                    exchange_drain(old)
                for gather in gathers:
                    gather.drain()
                gathers = []
                exchange_start(turn, field)
        else:
            load_l.wait()

        def before(r):
            value = loads[r, :] - field[r, :]
            field[r, :] = value
            h, l = split(value)
            both[r, 0:cases] = h
            both[r, cases : 2 * cases] = l

        with jax.named_scope("before"):
            by_rows(unknowns, 128, before)
            early[...] = product(t_high[...], t_low[...], both)
        with jax.named_scope("xwait"):
            exchange_wait(turn)
        with jax.named_scope("term"):
            split_beside(arrived[turn], edge_both)
            mine = pl.multiple_of(me * primal, primal)
            term_all[slot, pl.ds(mine, primal), :] = early[...] - product(p_high[...], p_low[...], edge_both)
        terms = Halves(grid, term_all.at[slot], primal, term_send, term_recv)
        with jax.named_scope("termstart"):
            terms.start()
        gathers.append(terms)

        def settle(r):
            value = field[r, :] - moved(r)
            residual[r, :] = value
            h, l = split(weight[r, :] * value)
            both[r, 0:cases] = h
            both[r, cases : 2 * cases] = l

        if iteration == 0:
            with jax.named_scope("spread"):
                slot_rows[...] = jnp.full(slot_rows.shape, -1, jnp.int32)
                for d in range(6):
                    slot_rows[:, d * face : (d + 1) * face] = slot_lists[d]
                hits = slot_rows[...]
                tile = tile_of(unknowns, 64)

                def mark(i, carry):
                    r = pl.ds(pl.multiple_of(i * tile, tile), tile)
                    row = lax.broadcasted_iota(jnp.int32, (tile, edge), 0) + i * tile
                    spread[r, :] = jnp.where(row == hits, 1.0, 0.0).astype(jnp.bfloat16)
                    return carry

                lax.fori_loop(0, unknowns // tile, mark, 0)
                corrected[...] = jnp.zeros_like(corrected)
        with jax.named_scope("settle"):
            by_rows(unknowns, 512, settle)
        if iteration == ITERS - 1:
            out_residual = pltpu.make_async_copy(residual, residual_out, out_sem.at[0])
            out_residual.start()

        def invert(r):
            local[r, :] = weight[r, :] * product(b_high[r, :], b_low[r, :], both)

        def inverts(i):
            def run():
                with jax.named_scope("invert"):
                    invert(pl.ds(i * chunk, chunk))

            return run

        def splits(i):
            def run():
                with jax.named_scope("splitb"):
                    if i == 0:
                        load_b.wait()
                    r = pl.ds(i * chunk, chunk)
                    split_rows(full.at[r], b_high.at[r], b_low.at[r])

            return run

        def turn_coarse():
            with jax.named_scope("transc"):
                load_c.wait()
                for k in range(0, coarse_own.shape[1], 128):
                    coarse_t[k : k + 128, :] = coarse_own[:, k : k + 128].T

        def read_maps():
            with jax.named_scope("maps"):
                if grid.count > 1:
                    block = map_all.at[pl.ds(0, grid.count - 1)]
                    pltpu.make_async_remote_copy(
                        src_ref=block, dst_ref=block, send_sem=map_send, recv_sem=map_recv,
                        device_id=grid.c, device_id_type=MESH,
                    ).wait()
                to_scalars.start()

        def pick(p, carry):
            take_rows(picked, coarse_t, all_map.at[p, 0], primal)
            h, l = split(picked[...].T)
            k = pl.ds(pl.multiple_of(p * primal, primal), primal)
            c_high[:, k] = h
            c_low[:, k] = l
            return carry

        plane = grid.count // sizes[0]
        width = plane * primal
        coarse_tile = term_both.shape[0]
        mine = pl.multiple_of(me * own, own)
        sol_all[iteration][pl.ds(mine, own), :] = jnp.zeros((own, cases), jnp.float32)

        def plane_of(head):
            return grid.line[head]

        def picks(head, part, parts):
            def run():
                with jax.named_scope("pick"):
                    if head == 0 and part == 0:
                        to_scalars.wait()
                    first = plane_of(head) * plane
                    lax.fori_loop(first + plane * part // parts, first + plane * (part + 1) // parts, pick, 0)

            return run

        def collects(d):
            def run():
                with jax.named_scope("clocal"):
                    collect(1, local, d)

            return run

        if iteration == 0:
            read_maps()
            first = [turn_coarse] + [picks(head, part, 4) for head in range(sizes[0]) for part in range(4)]
            work = [splits(i) for i in range(chunks)]
        else:
            first, work = [], []
        def send_local():
            with jax.named_scope("xlocal"):
                for d in range(6):
                    dispatch(1, d)

        work += [inverts(i) for i in range(chunks)] + [collects(d) for d in range(6)]

        def after_plane(head):
            def coarse(i, carry):
                k = pl.ds(pl.multiple_of(plane_of(head) * width + i * coarse_tile, coarse_tile), coarse_tile)
                split_beside(term_all.at[slot, k], term_both)
                sol_all[iteration][pl.ds(mine, own), :] += product(c_high[:, k], c_low[:, k], term_both)
                return carry

            with jax.named_scope("coarse"):
                lax.fori_loop(0, width // coarse_tile, coarse, 0)

        with jax.named_scope("termfin"):
            terms.finish(first, work, after_plane)
        sols = Halves(grid, sol_all[iteration], own, sol_send, sol_recv)
        with jax.named_scope("solstart"):
            sols.start()
        gathers.append(sols)

        send_local()

        def approach(r):
            solution[r, :] = solution[r, :] + damping * (local[r, :] + moved(r))

        def approaches(i):
            def run():
                with jax.named_scope("approach"):
                    if i == 0:
                        exchange_wait(1)
                        split_beside(arrived[1], edge_both)
                    approach(pl.ds(i * chunk, chunk))

            return run

        def shapes():
            with jax.named_scope("shapes"):
                exchange_wait(shape_turn)
                split_rows(arrived[shape_turn], n_high, n_low)

        work = ([shapes] if iteration == 0 else []) + [pause] * sols.waits(1) + [approaches(i) for i in range(chunks)]
        with jax.named_scope("solfin"):
            sols.finish((), work)
        with jax.named_scope("take"):
            take_rows(coarse_rows, sol_all[iteration], all_map.at[me, 0], primal)
            split_beside(coarse_rows, sol_both)
            for d in range(6):

                @pl.when(exists(d))
                def _():
                    q = neighbour(d)
                    r = slice(d * face, (d + 1) * face)
                    take_rows(coarse_rows, sol_all[iteration], all_map.at[q, 0], primal)
                    split_beside(coarse_rows, term_both.at[0:primal])
                    corrected[r, :] = product(n_high[r, :], n_low[r, :], term_both.at[0:primal])

            split_beside(corrected, edge_both)

        def advance(r):
            change = product(m_high[r, :], m_low[r, :], sol_both) + moved(r)
            value = solution[r, :] + damping * change
            solution[r, :] = value
            if iteration < ITERS - 1:
                h, l = split(value)
                both[r, 0:cases] = h
                both[r, cases : 2 * cases] = l

        with jax.named_scope("advance"):
            if iteration < ITERS - 1:
                by_rows(unknowns, 512, advance)
            else:
                for i in range(chunks):
                    r = pl.ds(i * chunk, chunk)
                    advance(r)
                    out_solution[i].start()
    with jax.named_scope("out"):
        for turn in range(3):
            exchange_drain(turn)
        for gather in gathers:
            gather.drain()
        out_residual.wait()
        for each in out_solution:
            each.wait()


def settle_outputs(first_in, second_in, first_out, second_out, stage, come, go):
    pairs = ((first_in, first_out), (second_in, second_out))
    pieces = stage.shape[1]
    rows = stage.shape[2]
    entering, leaving = [], []
    for i in range(pieces):
        for k, (source, target) in enumerate(pairs):
            r = pl.ds(i * rows, rows)
            entering.append(pltpu.make_async_copy(source.at[r], stage.at[k, i], come.at[k, i]))
            leaving.append(pltpu.make_async_copy(stage.at[k, i], target.at[r], go.at[k, i]))
    for each in entering:
        each.start()
    for a, b in zip(entering, leaving):
        a.wait()
        b.start()
    for each in leaving:
        each.wait()


def body(sizes, loads, start, schur, inv_local, basis, coarse_inv, face_index, multiplicity, primal_map):
    unknowns, cases = loads.shape[3:]
    face = face_index.shape[4]
    primal = basis.shape[4]
    count = sizes[0] * sizes[1] * sizes[2]
    total = coarse_inv.shape[1]
    own = coarse_inv.shape[0] // sizes[2]
    edge = -(-6 * face // 128) * 128
    anywhere = pl.BlockSpec(memory_space=pl.ANY)
    dma = pltpu.SemaphoreType.DMA
    f32, bf16 = jnp.float32, jnp.bfloat16
    turns = 3
    coarse_tile = tile_of(count // sizes[0] * primal, 1024)
    grid_stages = stages_of(sizes)
    landings = max(arrivals(grid_stages), arrivals((grid_stages[0], grid_stages[2], grid_stages[1], grid_stages[3])))
    term_slots = ITERS if ITERS * count * primal <= 8 * unknowns else 1
    vec = pltpu.VMEM((unknowns, cases), f32)
    out = jax.ShapeDtypeStruct((unknowns, cases), f32)
    lists = face_index.reshape(6, 1, face)
    solution, residual = pl.pallas_call(
        functools.partial(main_kernel, sizes, face),
        out_shape=(out, out),
        in_specs=[anywhere] * 9,
        out_specs=(anywhere, anywhere),
        scratch_shapes=[
            pltpu.SMEM((6, 1, face), jnp.int32),
            pltpu.VMEM((6, 1, face), jnp.int32),
            pltpu.VMEM((1, unknowns), jnp.int32),
            pltpu.VMEM((unknowns, unknowns), f32),
            pltpu.VMEM((unknowns, unknowns), bf16),
            pltpu.VMEM((unknowns, unknowns), bf16),
            pltpu.VMEM((unknowns, unknowns), bf16),
            pltpu.VMEM((unknowns, unknowns), bf16),
            pltpu.VMEM((unknowns, primal), bf16),
            pltpu.VMEM((unknowns, primal), bf16),
            pltpu.VMEM((primal, unknowns), bf16),
            pltpu.VMEM((primal, unknowns), bf16),
            pltpu.VMEM((primal, edge), bf16),
            pltpu.VMEM((primal, edge), bf16),
            pltpu.VMEM((edge, primal), bf16),
            pltpu.VMEM((edge, primal), bf16),
            pltpu.VMEM((own, count * primal), bf16),
            pltpu.VMEM((own, count * primal), bf16),
            pltpu.VMEM((own, total), f32),
            pltpu.VMEM((total, own), f32),
            pltpu.VMEM((count, 1, primal), jnp.int32),
            pltpu.SMEM((count, 1, primal), jnp.int32),
            pltpu.VMEM((primal, own), f32),
            pltpu.VMEM((1, edge), jnp.int32),
            pltpu.VMEM((unknowns, edge), bf16),
            vec, vec, pltpu.VMEM((unknowns, primal), f32), vec, vec, vec, vec,
            pltpu.VMEM((primal, cases), f32),
            pltpu.VMEM((unknowns, 2 * cases), bf16),
            pltpu.VMEM((edge, 2 * cases), bf16),
            pltpu.VMEM((coarse_tile, 2 * cases), bf16),
            pltpu.VMEM((primal, 2 * cases), bf16),
            pltpu.VMEM((primal, cases), f32),
            pltpu.VMEM((edge, cases), f32),
            pltpu.VMEM((turns, edge, cases), f32),
            [pltpu.VMEM((edge, cases), f32) for _ in range(turns)],
            pltpu.VMEM((term_slots, count * primal, cases), f32),
            [pltpu.VMEM((total, cases), f32) for _ in range(ITERS)],
            dma((11 + unknowns // tile_of(unknowns, 256),)), dma((1 + unknowns // tile_of(unknowns, 256),)),
            dma(()), dma(()),
            dma((turns, 6)), dma((turns, 6)),
            dma((2,)), dma((2, landings)),
            dma((2,)), dma((2, landings)),
        ],
        compiler_params=pltpu.CompilerParams(
            collective_id=1, has_side_effects=True, vmem_limit_bytes=67043328
        ),
    )(
        lists, multiplicity.reshape(1, unknowns), primal_map.reshape(1, primal),
        loads.reshape(unknowns, cases), start.reshape(unknowns, cases), basis.reshape(unknowns, primal),
        schur.reshape(unknowns, unknowns), inv_local.reshape(unknowns, unknowns), coarse_inv,
    )
    pieces = 2
    rows = unknowns // pieces
    solution, residual = pl.pallas_call(
        settle_outputs,
        out_shape=(out, out),
        in_specs=[anywhere] * 2,
        out_specs=(anywhere, anywhere),
        scratch_shapes=[pltpu.VMEM((2, pieces, rows, cases), f32), dma((2, pieces)), dma((2, pieces))],
    )(solution, residual)
    return (solution.reshape(loads.shape), residual.reshape(loads.shape))


def solution(mesh):
    sizes = tuple(mesh.shape[a] for a in AXES)
    field = P("gx", "gy", "gz", None, None)
    placed = (field,) * 5 + (P(("gx", "gy"), None), field, P("gx", "gy", "gz", None), P("gx", "gy", "gz", None))
    return jax.shard_map(
        functools.partial(body, sizes),
        mesh=mesh,
        in_specs=placed,
        out_specs=(field, field),
        check_vma=False,
    )
```
